256 devices in a mesh: rows: 32 (over z_hi, y, core), rep: 8 (over z_lo, x).
Axes of the slice: x: 4, y: 4, z: 8 (z_hi: 4, z_lo: 2; z = z_hi * 2 + z_lo), core: 2. Of those that a mesh axis runs over, the one named last changes fastest.
Arguments:
- features: bfloat16 [32768, 256], P('rows'), may hold values from -6 to 6
- inv_sqrt_degree: bfloat16 [32768], P('rows'), may hold values from 0.25 to 1
- weight: bfloat16 [256, 256], replicated, may hold values from -0.375 to 0.375
- tile_vals: bfloat16 [32, 1024, 128, 128], P('rows', 'rep'), may hold values from -0.046875 to 0.046875
- tile_row: int32 [32, 1024], P('rows', 'rep'), may hold values from 0 to 7, as said below
- tile_col: int32 [32, 1024], P('rows', 'rep'), may hold values from 0 to 31, as said below
- tile_count: int32 [32, 32], P('rows', 'rep'), may hold values from 0 to 64, as said below
- cotangent: bfloat16 [32768, 256], P('rows'), may hold values from -6 to 6
Outputs:
- activated: bfloat16 [32768, 256], P(('rows', 'rep'))
- weight_grad: float32 [256, 256], replicated
- feature_grad: bfloat16 [32768, 256], P(('rep', 'rows'))
The draws below stay inside these ranges and needn't reach their ends.
Inputs may be any that keep to these rules, and one draw needn't show every extreme that they name: `tile_count`: each count is at most 64; the 4 counts of row block i and columns r * 4 .. r * 4 + 3 sum to at most 128. Some pair holds exactly 64 tiles and some block row and replica exactly 128, in every draw. `tile_row`: the valid slots of a block row and replica are ordered by column block, and inside one block pair their positions are distinct. A valid slot counted for column block r * 4 + s has tile_col between s * 8 and s * 8 + 7.
All inputs are finite; a program needn't handle non-finite values.
Results may differ from the reference program's by a relative error of at most 0.015.
Values may be sent and summed in bfloat16 or wider, within the bound.
No kernel may reach another device: no remote copies, remote signals or barrier semaphores. Data moves between devices by JAX's collectives and lax.ppermute only.
A program may use at most 128 MiB of HBM per device.

```python
import math
import jax
import jax.numpy as jnp
from jax import lax

F = 256
TS = 128
SECTIONS = 4
TB = 8
KB = 64
KT = 128
TILES = 1024
NODES = 32768
N_ROWS = 32
N_REP = 8


def tile_layout(key):
    base = jax.random.fold_in(key, 11)
    k_heavy, k_raw, k_pick, k_perm, k_junk_row, k_junk_col = jax.random.split(base, 6)
    devices = N_ROWS * N_REP
    heavy = jax.random.randint(k_heavy, (N_ROWS, 1, 1), 1, 5)
    raw = jax.random.randint(k_raw, (N_ROWS, N_REP, SECTIONS), 0, KB + 1) * heavy // 4
    raw = raw.reshape(devices, SECTIONS).astype(jnp.int32)
    section_ids = jnp.arange(SECTIONS, dtype=jnp.int32)
    filled = jnp.clip(KT - section_ids * KB, 0, KB).astype(jnp.int32)
    chosen = jax.random.randint(k_pick, (), 0, devices)
    device_ids = jnp.arange(devices, dtype=jnp.int32)
    raw = jnp.where((device_ids == chosen)[:, None], filled[None, :], raw)
    totals = jnp.sum(raw, axis=1, keepdims=True)
    counts = (raw * KT // jnp.maximum(totals, KT)).astype(jnp.int32)
    ends = jnp.cumsum(counts, axis=1).astype(jnp.int32)
    starts = ends - counts
    slot_ids = jnp.arange(KT, dtype=jnp.int32)
    section_of = jnp.sum((slot_ids[None, :, None] >= ends[:, None, :]).astype(jnp.int32), axis=2)
    section_of = jnp.minimum(section_of, SECTIONS - 1).astype(jnp.int32)
    start_of = jnp.take_along_axis(starts, section_of, axis=1)
    within = jnp.clip(slot_ids[None, :] - start_of, 0, KB - 1)
    perm_keys = jax.random.split(k_perm, devices * SECTIONS)
    perms = jax.vmap(lambda one_key: jax.random.permutation(one_key, KB))(perm_keys)
    perms = perms.reshape(devices, SECTIONS, KB).astype(jnp.int32)
    position = perms[device_ids[:, None], section_of, within]
    valid = slot_ids[None, :] < ends[:, -1:]
    junk_row = jax.random.randint(k_junk_row, (devices, KT), 0, TB)
    junk_col = jax.random.randint(k_junk_col, (devices, KT), 0, SECTIONS * TB)
    rows = jnp.where(valid, position // TB, junk_row).astype(jnp.int32)
    cols = jnp.where(valid, section_of * TB + position % TB, junk_col).astype(jnp.int32)
    return (counts.reshape(N_ROWS, N_ROWS), rows.reshape(N_ROWS, TILES), cols.reshape(N_ROWS, TILES))


def draw_tile_count(key, part):
    return tile_layout(key)[0]


def draw_tile_row(key, part):
    return tile_layout(key)[1]


def draw_tile_col(key, part):
    return tile_layout(key)[2]


def levels(own_key, dims, shards, smallest, high):
    level = 1.0
    for axis_at, parts in shards:
        draws = jax.random.uniform(jax.random.fold_in(jax.random.fold_in(own_key, 6), axis_at), (parts,), jnp.float32, smallest / len(shards), high / len(shards))
        level = level * jnp.repeat(jnp.exp(draws), dims[axis_at] // parts).reshape((-1,) + (1,) * (len(dims) - 1 - axis_at))
    return level


def normal_values(stream_key, extent, scale, most, shards=(), held_as=jnp.bfloat16):
    result = jax.random.normal(stream_key, extent, jnp.float32) * scale
    if len(shards) > 0:
        result = levels(stream_key, extent, shards, -0.22, 0.18) * result
    return jnp.clip(result, min=-most, max=most).astype(held_as)


def setup_inputs(seed: int = 0) -> dict:
    key_list = jax.random.split(jax.random.key(seed), 9)
    return {
        "features": normal_values(key_list[0], (NODES, F), 1.0, 6.0, ((0, 32),)),
        "inv_sqrt_degree": jnp.clip(jnp.exp(math.log(1.0) - 1.3862944 * jax.random.uniform(key_list[1], (NODES,), jnp.float32) ** levels(key_list[1], (NODES,), ((0, 32),), -0.2, 0.2)), 0.25, 1.0).astype(jnp.bfloat16),
        "weight": normal_values(key_list[2], (F, F), F ** -0.5, 0.375),
        "tile_vals": normal_values(key_list[3], (N_ROWS, TILES, TS, TS), (N_REP * KT * TS // TB) ** -0.5, 0.046875, ((0, 32), (1, 8))),
        "tile_row": draw_tile_row(jax.random.fold_in(key_list[8], 71), 0),
        "tile_col": draw_tile_col(jax.random.fold_in(key_list[8], 71), 0),
        "tile_count": draw_tile_count(jax.random.fold_in(key_list[8], 71), 0),
        "cotangent": normal_values(key_list[7], (NODES, F), 1.0, 6.0, ((0, 32),)),
    }


def reference(features, inv_sqrt_degree, weight, tile_vals, tile_row, tile_col, tile_count, cotangent):
    devices = N_ROWS * N_REP
    nodes = features.shape[0]
    width = features.shape[1]
    tile = tile_vals.shape[-1]
    per_block = nodes // N_ROWS // tile
    slots = tile_vals.shape[1] // N_REP
    sections = N_ROWS // N_REP
    degree = inv_sqrt_degree.astype(jnp.float32)[:, None]
    scaled = (degree * features.astype(jnp.float32)).astype(jnp.bfloat16)
    values = tile_vals.reshape(devices, slots, tile, tile)
    rows_local = tile_row.reshape(devices, slots).astype(jnp.int32)
    cols_local = tile_col.reshape(devices, slots).astype(jnp.int32)
    totals = lax.optimization_barrier(jnp.sum(tile_count.reshape(devices, sections), axis=1)).astype(jnp.int32)
    device_ids = jnp.arange(devices, dtype=jnp.int32)
    out_tile = (device_ids // N_REP * per_block)[:, None] + rows_local
    in_tile = (device_ids % N_REP * (sections * per_block))[:, None] + cols_local
    keep = jnp.arange(slots, dtype=jnp.int32)[None, :] < totals[:, None]
    source_tiles = scaled.reshape(nodes // tile, tile, width)

    def forward_step(carry, item):
        vals, out_t, in_t, keep_d = item
        prod = jnp.einsum('kij,kjf->kif', vals.astype(jnp.float32), source_tiles[in_t].astype(jnp.float32))
        prod = jnp.where(keep_d[:, None, None], prod, jnp.float32(0.0))
        return (carry.at[out_t].add(prod), None)
    start = jnp.zeros((nodes // tile, tile, width), jnp.float32)
    summed, _ = lax.scan(forward_step, start, (values, out_tile, in_tile, keep))
    propagated = (degree * (summed.reshape(nodes, width) + scaled.astype(jnp.float32))).astype(jnp.bfloat16)
    preact = jnp.dot(propagated, weight, preferred_element_type=jnp.float32)
    gate = jax.nn.sigmoid(preact)
    activated = (preact * gate).astype(jnp.bfloat16)
    grad_pre = (cotangent.astype(jnp.float32) * gate * (1.0 + preact * (1.0 - gate))).astype(jnp.bfloat16)
    weight_grad = jnp.dot(propagated.T, grad_pre, preferred_element_type=jnp.float32) * jnp.float32(nodes ** (-0.5))
    back = (degree * jnp.dot(grad_pre, weight.T, preferred_element_type=jnp.float32)).astype(jnp.bfloat16)
    back_tiles = back.reshape(nodes // tile, tile, width)

    def backward_step(carry, item):
        vals, out_t, in_t, keep_d = item
        prod = jnp.einsum('kji,kjf->kif', vals.astype(jnp.float32), back_tiles[out_t].astype(jnp.float32))
        prod = jnp.where(keep_d[:, None, None], prod, jnp.float32(0.0))
        return (carry.at[in_t].add(prod), None)
    gathered, _ = lax.scan(backward_step, start, (values, out_tile, in_tile, keep))
    feature_grad = (degree * (gathered.reshape(nodes, width) + back.astype(jnp.float32))).astype(jnp.bfloat16)
    return (activated, weight_grad, feature_grad)
```

```python
import jax
import jax.numpy as jnp
from jax import lax
from jax.experimental import pallas as pl
from jax.experimental.pallas import tpu as pltpu
from jax.sharding import Mesh, PartitionSpec as P

ZH, Y, C, ZL, X = 4, 4, 2, 2, 4
ROWS = ("zh", "y", "c")
REP = ("zl", "x")
ALL = ROWS + REP
TILE = 128


def flat(zh, y, c, zl, x):
    return (((zh * Y + y) * C + c) * ZL + zl) * X + x


def chunk_route(m):
    pairs = []
    for j in range(ZH * Y * C):
        for k in range(ZL * X):
            r = j // 4
            source = j * (ZL * X) + k
            target = flat((j % 4) ^ m, k // 2, k % 2, r // X, r % X)
            pairs.append((source, target))
    return pairs


def assemble_body(count, row, pos, vals, own, other, sem):
    own[...] = jnp.zeros_like(own)
    other[...] = jnp.zeros_like(other)
    total = count[0]

    def place(k, into):
        at = pos[k] % 16
        return pltpu.make_async_copy(
            vals.at[k],
            into.at[pl.ds(pl.multiple_of(row[k] * TILE, TILE), TILE),
                    pl.ds(pl.multiple_of(at * TILE, TILE), TILE)],
            sem.at[k],
        )

    @pl.loop(0, total)
    def _(k):
        @pl.when(pos[k] < 16)
        def _():
            place(k, own).start()

        @pl.when(pos[k] >= 16)
        def _():
            place(k, other).start()

    @pl.loop(0, total)
    def _(k):
        place(k, own).wait()


def assemble(count, row, pos, vals, rows, cols):
    half = jax.ShapeDtypeStruct((rows, cols), jnp.bfloat16)
    smem = pl.BlockSpec(memory_space=pltpu.SMEM)
    whole = pl.BlockSpec(memory_space=pltpu.VMEM)
    return pl.pallas_call(
        assemble_body,
        out_shape=(half, half),
        in_specs=[smem, smem, smem, pl.BlockSpec(memory_space=pltpu.HBM)],
        out_specs=(whole, whole),
        scratch_shapes=[pltpu.SemaphoreType.DMA((vals.shape[0],))],
        name="assemble",
    )(count, row, pos, vals)


def shards(features, inv_sqrt_degree, weight, tile_vals, tile_row, tile_col, tile_count, cotangent):
    bf16, f32 = jnp.bfloat16, jnp.float32
    nodes_block, width = features.shape
    zh, core = lax.axis_index("zh"), lax.axis_index("c")
    replica = lax.axis_index(REP)
    share = nodes_block // (ZL * X)
    nodes = nodes_block * ZH * Y * C
    start = replica * share
    deg_bf = lax.dynamic_slice_in_dim(inv_sqrt_degree, start, share, 0)
    deg = deg_bf.astype(f32)[:, None]
    feats = lax.dynamic_slice_in_dim(features, start, share, 0)
    cot = lax.dynamic_slice_in_dim(cotangent, start, share, 0).astype(f32)
    scaled = (deg * feats.astype(f32)).astype(bf16)
    deg_rows = jnp.pad(deg_bf[None, :], ((0, 15), (0, width - share)))
    sent = [jnp.concatenate([scaled, deg_rows], 0), scaled, scaled, scaled]
    got = [lax.ppermute(sent[m], ALL, chunk_route(m)) for m in range(4)]

    section, sub = tile_col[0] // 8, tile_col[0] % 8
    pos = ((sub % 2) ^ core) * 16 + (sub // 2) * 4 + (section ^ zh)
    total = jnp.sum(tile_count[0]).reshape(1)
    own_a, other_a = assemble(
        total.astype(jnp.int32), tile_row[0], pos.astype(jnp.int32), tile_vals[0], nodes_block, Y * 4 * TILE
    )

    chunk_deg = got[0][share, :share].astype(f32)[:, None]
    piece = jnp.concatenate([got[0][:share], got[1], got[2], got[3]], 0)
    gathered = lax.all_to_all(jnp.broadcast_to(piece[None], (Y, 4 * share, width)), "y", 0, 0)
    own_x = gathered.reshape(Y * 4 * share, width)
    swap = [(0, 1), (1, 0)]
    other_x = lax.ppermute(own_x, "c", swap)
    partial = jnp.dot(own_a, own_x, preferred_element_type=f32) + jnp.dot(
        other_a, other_x, preferred_element_type=f32
    )
    parts = lax.all_to_all(partial.astype(bf16).reshape(ZL * X, share, width), REP, 0, 0)
    summed = jnp.sum(parts.astype(f32), 0)

    propagated = (deg * (summed + scaled.astype(f32))).astype(bf16)
    preact = jnp.dot(propagated, weight, preferred_element_type=f32)
    gate = jax.nn.sigmoid(preact)
    activated = (preact * gate).astype(bf16)
    grad_pre = (cot * gate * (1.0 + preact * (1.0 - gate))).astype(bf16)
    back = (
        deg * lax.dot_general(grad_pre, weight, (((1,), (1,)), ((), ())), preferred_element_type=f32)
    ).astype(bf16)
    local_grad = lax.dot_general(
        propagated, grad_pre, (((0,), (0,)), ((), ())), preferred_element_type=f32
    ) * (float(nodes) ** -0.5)

    slices = local_grad.astype(bf16).reshape(ZL * X, width // (ZL * X), width)
    both = jnp.concatenate([jnp.broadcast_to(back[None], (ZL * X, share, width)), slices], 1)
    both = lax.all_to_all(both, REP, 0, 0)
    back_block = both[:, :share].reshape(nodes_block, width)
    w_slice = jnp.sum(both[:, share:].astype(f32), 0)
    w_slice = w_slice + lax.ppermute(w_slice, "c", swap)

    def pull(a):
        return lax.dot_general(a, back_block, (((0,), (0,)), ((), ())), preferred_element_type=f32)

    other_g = lax.ppermute(pull(other_a).astype(bf16), "c", swap)
    col_sum = (pull(own_a) + other_g.astype(f32)).astype(bf16).reshape(Y, 4 * share, width)
    w_rows = w_slice.astype(bf16)
    both = lax.all_to_all(
        jnp.concatenate([col_sum, jnp.broadcast_to(w_rows[None], (Y,) + w_rows.shape)], 1), "y", 0, 0
    )
    both = jnp.sum(both.astype(f32), 0)
    chunks, w_rows = both[: 4 * share].reshape(4, share, width), both[4 * share :]
    w_sum = w_rows
    grad = chunks[0]
    for m in range(1, 4):
        pairs = [(i, i ^ m) for i in range(ZH)]
        payload = jnp.concatenate([chunks[m], w_rows], 0).astype(bf16)
        came = lax.ppermute(payload, "zh", pairs).astype(f32)
        grad = grad + came[:share]
        w_sum = w_sum + came[share:]
    own_back = lax.ppermute(back, ALL, chunk_route(0)).astype(f32)
    feature_grad = (chunk_deg * (grad + own_back)).astype(bf16)
    weight_grad = lax.all_to_all(jnp.broadcast_to(w_sum[None], (ZL * X,) + w_sum.shape), REP, 0, 0)
    return (activated, weight_grad.reshape(width, width), feature_grad)


def solution(mesh):
    fine = Mesh(mesh.devices.reshape(ZH, Y, C, ZL, X), ALL)
    placed = (
        P(ROWS, None),
        P(ROWS),
        P(),
        P(ROWS, REP, None, None),
        P(ROWS, REP),
        P(ROWS, REP),
        P(ROWS, REP),
        P(ROWS, None),
    )
    return jax.shard_map(
        shards,
        mesh=fine,
        in_specs=placed,
        out_specs=(P(ALL, None), P(), P(REP + ROWS, None)),
        check_vma=False,
    )
```

```python
import jax
import jax.numpy as jnp
from jax import lax
from jax.experimental import pallas as pl
from jax.experimental.pallas import tpu as pltpu
from jax.sharding import Mesh, PartitionSpec as P

ZH, Y, C, ZL, X = 4, 4, 2, 2, 4
ROWS = ("zh", "y", "c")
REP = ("zl", "x")
ALL = ROWS + REP
TILE = 128


def flat(zh, y, c, zl, x):
    return (((zh * Y + y) * C + c) * ZL + zl) * X + x


def piece_route():
    pairs = []
    for j in range(ZH * Y * C):
        for k in range(ZL * X):
            zl, x = k // X, k % X
            r = j // 4
            pairs.append((j * (ZL * X) + k, flat(zl * 2 + x % 2, j % 4, x // 2, r // X, r % X)))
    return pairs


def share_route():
    pairs = []
    for j in range(ZH * Y * C):
        for k in range(ZL * X):
            r = j // 4
            pairs.append((j * (ZL * X) + k, flat(j % 4, k // 2, k % 2, r // X, r % X)))
    return pairs


def assemble_body(count, core, row, col, vals, own, other, sem):
    own[...] = jnp.zeros_like(own)
    other[...] = jnp.zeros_like(other)
    total = count[0, 0] + count[0, 1] + count[0, 2] + count[0, 3]

    @pl.loop(0, total)
    def _(k):
        at = col[0, k]
        sub = at % 8
        slot = (sub % 2) ^ core[0]
        place = (at // 8) * 4 + sub // 2
        down = pl.ds(pl.multiple_of(row[0, k] * TILE, TILE), TILE)
        across = pl.ds(pl.multiple_of(place * TILE, TILE), TILE)

        @pl.when(slot == 0)
        def _():
            pltpu.make_async_copy(vals.at[0, k], own.at[down, across], sem.at[k]).start()

        @pl.when(slot != 0)
        def _():
            pltpu.make_async_copy(vals.at[0, k], other.at[down, across], sem.at[k]).start()

    @pl.loop(0, total)
    def _(k):
        pltpu.make_async_copy(vals.at[0, k], own.at[pl.ds(0, TILE), pl.ds(0, TILE)], sem.at[k]).wait()


def assemble(count, core, row, col, vals, rows, cols):
    half = jax.ShapeDtypeStruct((rows, cols), jnp.bfloat16)
    smem = pl.BlockSpec(memory_space=pltpu.SMEM)
    whole = pl.BlockSpec(memory_space=pltpu.VMEM)
    return pl.pallas_call(
        assemble_body,
        out_shape=(half, half),
        in_specs=[smem, smem, smem, smem, pl.BlockSpec(memory_space=pltpu.HBM)],
        out_specs=(whole, whole),
        scratch_shapes=[pltpu.SemaphoreType.DMA((vals.shape[1],))],
        name="assemble",
    )(count, core, row, col, vals)


def shards(features, inv_sqrt_degree, weight, tile_vals, tile_row, tile_col, tile_count, cotangent):
    bf16, f32 = jnp.bfloat16, jnp.float32
    nodes_block, width = features.shape
    zh, core = lax.axis_index("zh"), lax.axis_index("c")
    replica = lax.axis_index(REP)
    reps = ZL * X
    share = nodes_block // reps
    nodes = nodes_block * ZH * Y * C
    half = lax.axis_index("x") // 2
    piece_rows = 4 * share
    feats = lax.dynamic_index_in_dim(features.reshape(4, 2, share, width), half, 1, False)
    degs = lax.dynamic_index_in_dim(inv_sqrt_degree.reshape(4, 2, share), half, 1, False)
    piece = (feats.astype(f32) * degs.astype(f32)[:, :, None]).astype(bf16).reshape(piece_rows, width)
    piece = lax.ppermute(piece, ALL, piece_route())

    own_a, other_a = assemble(
        tile_count, core.reshape(1), tile_row, tile_col, tile_vals, nodes_block, Y * piece_rows
    )
    start = replica * share
    deg_bf = lax.dynamic_slice_in_dim(inv_sqrt_degree, start, share, 0)
    deg_rows = jnp.pad(deg_bf[None, :], ((0, 15), (0, width - share)))
    deg = deg_bf.astype(f32)[:, None]
    scaled = (deg * lax.dynamic_slice_in_dim(features, start, share, 0).astype(f32)).astype(bf16)
    cot = lax.dynamic_slice_in_dim(cotangent, start, share, 0).astype(f32)
    piece, own_a, other_a, scaled, cot, deg_rows = lax.optimization_barrier(
        (piece, own_a, other_a, scaled, cot, deg_rows)
    )

    gathered = lax.all_to_all(jnp.broadcast_to(piece[None], (Y,) + piece.shape), "y", 0, 0)
    own_x = gathered.reshape(Y * piece_rows, width)
    swap = [(0, 1), (1, 0)]
    other_x = lax.ppermute(own_x, "c", swap)
    partial = jnp.dot(own_a, own_x, preferred_element_type=f32) + jnp.dot(
        other_a, other_x, preferred_element_type=f32
    )
    parts = lax.all_to_all(partial.astype(bf16).reshape(reps, share, width), REP, 0, 0)
    summed = jnp.sum(parts.astype(f32), 0)

    propagated = (deg * (summed + scaled.astype(f32))).astype(bf16)
    preact = jnp.dot(propagated, weight, preferred_element_type=f32)
    gate = jax.nn.sigmoid(preact)
    activated = (preact * gate).astype(bf16)
    grad_pre = (cot * gate * (1.0 + preact * (1.0 - gate))).astype(bf16)
    back = (
        deg * lax.dot_general(grad_pre, weight, (((1,), (1,)), ((), ())), preferred_element_type=f32)
    ).astype(bf16)
    local_grad = lax.dot_general(
        propagated, grad_pre, (((0,), (0,)), ((), ())), preferred_element_type=f32
    ) * (float(nodes) ** -0.5)

    back_sent = lax.ppermute(jnp.concatenate([back, deg_rows], 0), ALL, share_route())

    slices = local_grad.astype(bf16).reshape(reps, width // reps, width)
    both = jnp.concatenate([jnp.broadcast_to(back[None], (reps, share, width)), slices], 1)
    both = lax.all_to_all(both, REP, 0, 0)
    back_block = both[:, :share].reshape(nodes_block, width)
    w_slice = jnp.sum(both[:, share:].astype(f32), 0)
    w_slice = w_slice + lax.ppermute(w_slice, "c", swap)

    def pull(a):
        return lax.dot_general(a, back_block, (((0,), (0,)), ((), ())), preferred_element_type=f32)

    other_g = lax.ppermute(pull(other_a).astype(bf16), "c", swap)
    col_sum = (pull(own_a) + other_g.astype(f32)).astype(bf16)
    col_sum, back_sent = lax.optimization_barrier((col_sum, back_sent))
    col_sum = col_sum.reshape(4, 4, share, width).transpose(1, 0, 2, 3).reshape(Y, piece_rows, width)
    w_rows = w_slice.astype(bf16)
    both = lax.all_to_all(
        jnp.concatenate([col_sum, jnp.broadcast_to(w_rows[None], (Y,) + w_rows.shape)], 1), "y", 0, 0
    )
    both = jnp.sum(both.astype(f32), 0)
    chunks, w_rows = both[:piece_rows].reshape(4, share, width), both[piece_rows:]
    w_sum = w_rows
    grad = lax.dynamic_index_in_dim(chunks, zh, 0, False)
    for m in range(1, 4):
        pairs = [(i, i ^ m) for i in range(ZH)]
        chunk = lax.dynamic_index_in_dim(chunks, zh ^ m, 0, False)
        payload = jnp.concatenate([chunk, w_rows], 0).astype(bf16)
        came = lax.ppermute(payload, "zh", pairs).astype(f32)
        grad = grad + came[:share]
        w_sum = w_sum + came[share:]
    own_back = back_sent[:share].astype(f32)
    chunk_deg = back_sent[share, :share].astype(f32)[:, None]
    feature_grad = (chunk_deg * (grad + own_back)).astype(bf16)
    weight_grad = lax.all_to_all(jnp.broadcast_to(w_sum[None], (reps,) + w_sum.shape), REP, 0, 0)
    return (activated, weight_grad.reshape(width, width), feature_grad)


def solution(mesh):
    fine = Mesh(mesh.devices.reshape(ZH, Y, C, ZL, X), ALL)
    placed = (
        P(ROWS, None),
        P(ROWS),
        P(),
        P(ROWS, REP, None, None),
        P(ROWS, REP),
        P(ROWS, REP),
        P(ROWS, REP),
        P(ROWS, None),
    )
    return jax.shard_map(
        shards,
        mesh=fine,
        in_specs=placed,
        out_specs=(P(ALL, None), P(), P(REP + ROWS, None)),
        check_vma=False,
    )
```

```python
import jax
import jax.numpy as jnp
from jax import lax
from jax.experimental import pallas as pl
from jax.experimental.pallas import tpu as pltpu
from jax.sharding import Mesh, PartitionSpec as P

ZH, Y, C, ZL, X = 4, 4, 2, 2, 4
ROWS = ("zh", "y", "c")
REP = ("zl", "x")
ALL = ROWS + REP
TILE = 128


def flat(zh, y, c, zl, x):
    return (((zh * Y + y) * C + c) * ZL + zl) * X + x


def place_of(q, r):
    return (2 * (r % 2) + q // 2 + (q % 2) * (2 * (q // 2) - 1)) % Y


def piece_route():
    pairs = []
    for j in range(ZH * Y * C):
        for k in range(ZL * X):
            r = j // 4
            dx = (k % X - r % X) % X
            if k // X == r // X:
                near, far = 0, 3 if r // X == 0 else 1
            else:
                near, far = 1 if r // X == 0 else 3, 2
            zh = (j // (Y * C) + (far if dx < 2 else near)) % ZH
            pairs.append((j * (ZL * X) + k, flat(zh, place_of(j % 4, r), dx % 2, r // X, r % X)))
    return pairs


def return_route(m):
    pairs = []
    for zh in range(ZH):
        for q in range(4):
            for c in range(C):
                for r in range(ZL * X):
                    source = flat(zh, place_of(q, r), c, r // X, r % X)
                    pairs.append((source, flat(q, zh ^ m, c, r // X, r % X)))
    return pairs


def ring_route(back):
    pairs = []
    for y in range(Y):
        for c in range(C):
            step = 1 if (c == 0) != back else -1
            pairs.append((y * C + c, (y + step) % Y * C + c))
    return pairs


def share_route():
    pairs = []
    for j in range(ZH * Y * C):
        for k in range(ZL * X):
            r = j // 4
            pairs.append((j * (ZL * X) + k, flat(j % 4, k // 2, k % 2, r // X, r % X)))
    return pairs


def assemble_body(count, here, row, col, vals, own, other, sem):
    own[...] = jnp.zeros_like(own)
    other[...] = jnp.zeros_like(other)
    total = count[0, 0] + count[0, 1] + count[0, 2] + count[0, 3]

    @pl.loop(0, total)
    def _(k):
        at = col[0, k]
        q, sub = at >> 3, at & 7
        parity = sub & 1
        slot = parity ^ here[0]
        high, low = q >> 1, q & 1
        apart = (2 * here[2] + high + low * (2 * high - 1) - here[1]) & 3
        order = jnp.where((apart & 1) == 0, 3 * (apart >> 1), 1 + (((3 - apart) >> 1) ^ parity))
        place = order * 4 + (sub >> 1)
        down = pl.ds(pl.multiple_of(row[0, k] * TILE, TILE), TILE)
        across = pl.ds(pl.multiple_of(place * TILE, TILE), TILE)

        @pl.when(slot == 0)
        def _():
            pltpu.make_async_copy(vals.at[0, k], own.at[down, across], sem.at[k]).start()

        @pl.when(slot != 0)
        def _():
            pltpu.make_async_copy(vals.at[0, k], other.at[down, across], sem.at[k]).start()

    @pl.loop(0, total)
    def _(k):
        pltpu.make_async_copy(vals.at[0, k], own.at[pl.ds(0, TILE), pl.ds(0, TILE)], sem.at[k]).wait()


def assemble(count, here, row, col, vals, rows, cols):
    half = jax.ShapeDtypeStruct((rows, cols), jnp.bfloat16)
    smem = pl.BlockSpec(memory_space=pltpu.SMEM)
    whole = pl.BlockSpec(memory_space=pltpu.VMEM)
    return pl.pallas_call(
        assemble_body,
        out_shape=(half, half),
        in_specs=[smem, smem, smem, smem, pl.BlockSpec(memory_space=pltpu.HBM)],
        out_specs=(whole, whole),
        scratch_shapes=[pltpu.SemaphoreType.DMA((vals.shape[1],))],
        name="assemble",
    )(count, here, row, col, vals)


def shards(features, inv_sqrt_degree, weight, tile_vals, tile_row, tile_col, tile_count, cotangent):
    bf16, f32 = jnp.bfloat16, jnp.float32
    nodes_block, width = features.shape
    zh, y, core = lax.axis_index("zh"), lax.axis_index("y"), lax.axis_index("c")
    replica = lax.axis_index(REP)
    reps = ZL * X
    share = nodes_block // reps
    nodes = nodes_block * ZH * Y * C
    half = (lax.axis_index("x") + y // 2) % 2
    piece_rows = 4 * share
    feats = lax.dynamic_index_in_dim(features.reshape(4, 2, share, width), half, 1, False)
    degs = lax.dynamic_index_in_dim(inv_sqrt_degree.reshape(4, 2, share), half, 1, False)
    piece = (feats.astype(f32) * degs.astype(f32)[:, :, None]).astype(bf16).reshape(piece_rows, width)
    piece = lax.ppermute(piece, ALL, piece_route())

    own_a, other_a = assemble(
        tile_count, jnp.stack([core, y, replica % 2]), tile_row, tile_col, tile_vals, nodes_block, Y * piece_rows
    )
    start = replica * share
    deg_bf = lax.dynamic_slice_in_dim(inv_sqrt_degree, start, share, 0)
    deg_rows = jnp.pad(deg_bf[None, :], ((0, 15), (0, width - share)))
    deg = deg_bf.astype(f32)[:, None]
    scaled = (deg * lax.dynamic_slice_in_dim(features, start, share, 0).astype(f32)).astype(bf16)
    cot = lax.dynamic_slice_in_dim(cotangent, start, share, 0).astype(f32)
    piece, own_a, other_a, scaled, cot, deg_rows = lax.optimization_barrier(
        (piece, own_a, other_a, scaled, cot, deg_rows)
    )

    swap = [(0, 1), (1, 0)]
    ahead, behind = ring_route(False), ring_route(True)
    first = lax.ppermute(piece, ("y", "c"), ahead)
    second = lax.ppermute(piece, ("y", "c"), behind)
    third = lax.ppermute(first, ("y", "c"), ahead)
    partial = jnp.zeros((nodes_block, width), f32)
    for i, own_x in enumerate((piece, first, second, third)):
        other_x = lax.ppermute(own_x, "c", swap)
        at = slice(i * piece_rows, (i + 1) * piece_rows)
        partial = partial + jnp.dot(own_a[:, at], own_x, preferred_element_type=f32)
        partial = partial + jnp.dot(other_a[:, at], other_x, preferred_element_type=f32)
    parts = lax.all_to_all(partial.astype(bf16).reshape(reps, share, width), REP, 0, 0)
    summed = jnp.sum(parts.astype(f32), 0)

    propagated = (deg * (summed + scaled.astype(f32))).astype(bf16)
    preact = jnp.dot(propagated, weight, preferred_element_type=f32)
    gate = jax.nn.sigmoid(preact)
    activated = (preact * gate).astype(bf16)
    grad_pre = (cot * gate * (1.0 + preact * (1.0 - gate))).astype(bf16)
    back = (
        deg * lax.dot_general(grad_pre, weight, (((1,), (1,)), ((), ())), preferred_element_type=f32)
    ).astype(bf16)
    local_grad = lax.dot_general(
        propagated, grad_pre, (((0,), (0,)), ((), ())), preferred_element_type=f32
    ) * (float(nodes) ** -0.5)

    back_sent = lax.ppermute(jnp.concatenate([back, deg_rows], 0), ALL, share_route())

    slices = local_grad.astype(bf16).reshape(reps, width // reps, width)
    both = jnp.concatenate([jnp.broadcast_to(back[None], (reps, share, width)), slices], 1)
    both = lax.all_to_all(both, REP, 0, 0)
    back_block = both[:, :share].reshape(nodes_block, width)
    w_slice = jnp.sum(both[:, share:].astype(f32), 0)
    w_slice = w_slice + lax.ppermute(w_slice, "c", swap)

    w_rows = w_slice.astype(bf16)

    def pull(a, i):
        return lax.dot_general(
            a[:, i * piece_rows : (i + 1) * piece_rows],
            back_block,
            (((0,), (0,)), ((), ())),
            preferred_element_type=f32,
        )

    def both_rows(i):
        other_g = lax.ppermute(pull(other_a, i).astype(bf16), "c", swap)
        return pull(own_a, i) + other_g.astype(f32)

    def send(grad_rows, w_part, route):
        came = lax.ppermute(jnp.concatenate([grad_rows.astype(bf16), w_part], 0), ("y", "c"), route)
        return came[:piece_rows].astype(f32), came[piece_rows:]

    relayed, w_first = send(both_rows(3), w_rows, ahead)
    direct, w_second = send(both_rows(1), w_rows, behind)
    relayed, back_sent = lax.optimization_barrier((relayed, back_sent))
    relayed, w_third = send(both_rows(2) + relayed, w_first, ahead)
    chunks = (both_rows(0) + direct + relayed).astype(bf16).reshape(4, share, width)
    w_rows = sum(w.astype(f32) for w in (w_rows, w_first, w_second, w_third)).astype(bf16)
    grad = jnp.zeros((share, width), f32)
    w_sum = jnp.zeros(w_rows.shape, f32)
    for m in range(4):
        chunk = lax.dynamic_index_in_dim(chunks, zh ^ m, 0, False)
        came = lax.ppermute(jnp.concatenate([chunk, w_rows], 0), ALL, return_route(m)).astype(f32)
        grad = grad + came[:share]
        w_sum = w_sum + came[share:]
    own_back = back_sent[:share].astype(f32)
    chunk_deg = back_sent[share, :share].astype(f32)[:, None]
    feature_grad = (chunk_deg * (grad + own_back)).astype(bf16)
    weight_grad = lax.all_to_all(jnp.broadcast_to(w_sum[None], (reps,) + w_sum.shape), REP, 0, 0)
    return (activated, weight_grad.reshape(width, width), feature_grad)


def solution(mesh):
    fine = Mesh(mesh.devices.reshape(ZH, Y, C, ZL, X), ALL)
    placed = (
        P(ROWS, None),
        P(ROWS),
        P(),
        P(ROWS, REP, None, None),
        P(ROWS, REP),
        P(ROWS, REP),
        P(ROWS, REP),
        P(ROWS, None),
    )
    return jax.shard_map(
        shards,
        mesh=fine,
        in_specs=placed,
        out_specs=(P(ALL, None), P(), P(REP + ROWS, None)),
        check_vma=False,
    )
```

```python
import jax
import jax.numpy as jnp
from jax import lax
from jax.experimental import pallas as pl
from jax.experimental.pallas import tpu as pltpu
from jax.sharding import Mesh, PartitionSpec as P

ZH, Y, C, ZL, X = 4, 4, 2, 2, 4
ROWS = ("zh", "y", "c")
REP = ("zl", "x")
ALL = ROWS + REP
TILE = 128


def flat(zh, y, c, zl, x):
    return (((zh * Y + y) * C + c) * ZL + zl) * X + x


def place_of(q, r):
    return (2 * (r % 2) + q // 2 + (q % 2) * (2 * (q // 2) - 1)) % Y


def piece_route():
    pairs = []
    for j in range(ZH * Y * C):
        for k in range(ZL * X):
            r = j // 4
            dx = (k % X - r % X) % X
            if k // X == r // X:
                near, far = 0, 3 if r // X == 0 else 1
            else:
                near, far = 1 if r // X == 0 else 3, 2
            zh = (j // (Y * C) + (far if dx < 2 else near)) % ZH
            pairs.append((j * (ZL * X) + k, flat(zh, place_of(j % 4, r), dx % 2, r // X, r % X)))
    return pairs


def ring_route(back):
    pairs = []
    for y in range(Y):
        for c in range(C):
            step = 1 if (c == 0) != back else -1
            pairs.append((y * C + c, (y + step) % Y * C + c))
    return pairs


def order_of(apart, parity):
    return jnp.where((apart & 1) == 0, 3 * (apart >> 1), 1 + (((3 - apart) >> 1) ^ parity))


def apart_of(q, odd, y):
    high, low = q >> 1, q & 1
    return (2 * odd + high + low * (2 * high - 1) - y) & 3


def assemble_body(count, core, y, odd, row, col, vals, dense, sems):
    dense[...] = jnp.zeros_like(dense)
    total = count[0, 0] + count[0, 1] + count[0, 2] + count[0, 3]

    @pl.loop(0, total)
    def _(k):
        at = col[0, k]
        q, sub = at >> 3, at & 7
        parity, pair = sub & 1, sub >> 1
        place = (parity ^ core[0]) * 16 + order_of(apart_of(q, odd[0], y[0]), parity) * 4 + pair
        down = pl.ds(pl.multiple_of(row[0, k] * TILE, TILE), TILE)
        across = pl.ds(pl.multiple_of(place * TILE, TILE), TILE)
        pltpu.make_async_copy(vals.at[0, k], dense.at[down, across], sems.at[k]).start()

    @pl.loop(0, total)
    def _(k):
        corner = (pl.ds(0, TILE), pl.ds(0, TILE))
        pltpu.make_async_copy(vals.at[0, k], dense.at[corner], sems.at[k]).wait()


def assemble(count, core, y, odd, row, col, vals, rows, cols):
    smem = pl.BlockSpec(memory_space=pltpu.SMEM)
    return pl.pallas_call(
        assemble_body,
        out_shape=jax.ShapeDtypeStruct((rows, cols), jnp.bfloat16),
        in_specs=[smem] * 6 + [pl.BlockSpec(memory_space=pltpu.HBM)],
        out_specs=pl.BlockSpec(memory_space=pltpu.VMEM),
        scratch_shapes=[pltpu.SemaphoreType.DMA((vals.shape[1],))],
        name="assemble",
    )(count, core, y, odd, row, col, vals)


def regroup(ids, parity, rows, both, outs, others):
    y, odd, owner, q_own = ids
    for i, out in enumerate(outs):
        pair = (y + (0, 3 - 2 * parity, 1 + 2 * parity, 2)[i]) & 3

        def load(q, at):
            place = order_of(apart_of(q, odd, y), parity) * 4 + pair
            part = rows[pl.ds(pl.multiple_of(place * TILE, TILE), TILE), :]
            if others is None:
                return part
            return part + others[pl.ds(pl.multiple_of(i * 4 * TILE + at, TILE), TILE), :].astype(jnp.float32)

        for q in range(4):
            out[q * TILE : (q + 1) * TILE, :] = load(q, q * TILE).astype(out.dtype)

        @pl.when(owner != 0)
        def _():
            at = pl.multiple_of(q_own * TILE, TILE)
            mine = load(q_own, at) + both[2 * pair + parity, :TILE, :].astype(jnp.float32)
            out[pl.ds(at, TILE), :] = mine.astype(out.dtype)


def send_body(core, y, odd, owner, q_own, rows, both, out):
    outs = [out.at[i * 4 * TILE : (i + 1) * 4 * TILE] for i in range(4)]
    regroup((y[0], odd[0], owner[0], q_own[0]), 1 - core[0], rows, both, outs, None)


def keep_body(core, y, odd, owner, q_own, rows, both, others, out0, out1, out2, out3):
    ids = (y[0], odd[0], owner[0], q_own[0])
    regroup(ids, core[0], rows, both, (out0, out1, out2, out3), others)


def call_regroup(body, ids, arrays, outs, name):
    smem, whole = pl.BlockSpec(memory_space=pltpu.SMEM), pl.BlockSpec(memory_space=pltpu.VMEM)
    return pl.pallas_call(
        body,
        out_shape=outs,
        in_specs=[smem] * len(ids) + [whole] * len(arrays),
        out_specs=jax.tree.map(lambda _: whole, outs),
        compiler_params=pltpu.CompilerParams(vmem_limit_bytes=16 << 20),
        name=name,
    )(*ids, *arrays)


def shards(features, inv_sqrt_degree, weight, tile_vals, tile_row, tile_col, tile_count, cotangent):
    bf16, f32 = jnp.bfloat16, jnp.float32
    nodes_block, width = features.shape
    zh, y, core = lax.axis_index("zh"), lax.axis_index("y"), lax.axis_index("c")
    replica, block = lax.axis_index(REP), lax.axis_index(ROWS)
    reps = ZL * X
    share = nodes_block // reps
    nodes = nodes_block * ZH * Y * C
    half = (lax.axis_index("x") + y // 2) % 2
    piece_rows = 4 * share
    cols = 2 * Y * piece_rows
    feats = lax.dynamic_index_in_dim(features.reshape(4, 2, share, width), half, 1, False)
    degs = lax.dynamic_index_in_dim(inv_sqrt_degree.reshape(4, 2, share), half, 1, False)
    piece = (feats.astype(f32) * degs.astype(f32)[:, :, None]).astype(bf16).reshape(piece_rows, width)
    deg_rows = jnp.pad(degs.reshape(2, width), ((0, 14), (0, 0)))
    piece = lax.ppermute(jnp.concatenate([piece, deg_rows], 0), ALL, piece_route())

    ids = [core.reshape(1), y.reshape(1), (replica % 2).reshape(1)]
    dense = assemble(tile_count, *ids, tile_row, tile_col, tile_vals, nodes_block, cols)
    piece, dense = lax.optimization_barrier((piece, dense))

    swap = [(0, 1), (1, 0)]
    ahead, behind = ring_route(False), ring_route(True)
    first = lax.ppermute(piece, ("y", "c"), ahead)
    second = lax.ppermute(piece, ("y", "c"), behind)
    third = lax.ppermute(first, ("y", "c"), ahead)
    pieces = (piece, first, second, third)
    partial = jnp.zeros((nodes_block, width), f32)
    for i, own_x in enumerate(pieces):
        other_x = lax.ppermute(own_x[:piece_rows], "c", swap)
        at = slice(i * piece_rows, (i + 1) * piece_rows)
        partial = partial + jnp.dot(dense[:, at], own_x[:piece_rows], preferred_element_type=f32)
        at = slice((4 + i) * piece_rows, (5 + i) * piece_rows)
        partial = partial + jnp.dot(dense[:, at], other_x, preferred_element_type=f32)

    start = replica * share
    deg = lax.dynamic_slice_in_dim(inv_sqrt_degree, start, share, 0).astype(f32)[:, None]
    scaled = (deg * lax.dynamic_slice_in_dim(features, start, share, 0).astype(f32)).astype(bf16)
    cot = lax.dynamic_slice_in_dim(cotangent, start, share, 0).astype(f32)
    chunk_deg = lax.dynamic_slice(
        jnp.stack([p[piece_rows:] for p in pieces]),
        (order_of(apart_of(zh, replica % 2, y), core), y // 2, (y % 2) * share),
        (1, 1, share),
    ).reshape(share, 1).astype(f32)
    partial = partial.astype(bf16)
    partial, scaled, cot, chunk_deg = lax.optimization_barrier((partial, scaled, cot, chunk_deg))
    parts = lax.all_to_all(partial.reshape(reps, share, width), REP, 0, 0)
    summed = jnp.sum(parts.astype(f32), 0)

    propagated = (deg * (summed + scaled.astype(f32))).astype(bf16)
    preact = jnp.dot(propagated, weight, preferred_element_type=f32)
    gate = jax.nn.sigmoid(preact)
    activated = (preact * gate).astype(bf16)
    grad_pre = (cot * gate * (1.0 + preact * (1.0 - gate))).astype(bf16)
    back = (
        deg * lax.dot_general(grad_pre, weight, (((1,), (1,)), ((), ())), preferred_element_type=f32)
    ).astype(bf16)
    local_grad = lax.dot_general(
        propagated, grad_pre, (((0,), (0,)), ((), ())), preferred_element_type=f32
    ) * (float(nodes) ** -0.5)

    slices = local_grad.astype(bf16).reshape(reps, width // reps, width)
    both = jnp.concatenate([jnp.broadcast_to(back[None], (reps, share, width)), slices], 1)
    both = lax.all_to_all(both, REP, 0, 0)
    back_block = both[:, :share].reshape(nodes_block, width)
    w_sum = jnp.sum(both[:, share:].astype(f32), 0)
    ids = ids + [(replica == block // 4).astype(jnp.int32).reshape(1), (block % 4).reshape(1)]

    def pull(at):
        return lax.dot_general(
            dense[:, at], back_block, (((0,), (0,)), ((), ())), preferred_element_type=f32
        )

    other_g = call_regroup(
        send_body, ids, (pull(slice(cols // 2, cols)), both), pltpu.VMEM((cols // 2, width), bf16), "regroup_send"
    )
    other_g = lax.ppermute(other_g, "c", swap)
    own_rows = pull(slice(0, cols // 2))
    kinds = (f32, bf16, f32, bf16)
    keep, straight, aside, relay = call_regroup(
        keep_body,
        ids,
        (own_rows, both, other_g),
        tuple(pltpu.VMEM((piece_rows, width), kind) for kind in kinds),
        "regroup_keep",
    )
    relayed = lax.ppermute(relay, ("y", "c"), ahead).astype(f32)
    direct = lax.ppermute(straight, ("y", "c"), behind).astype(f32)
    w_sum = w_sum + lax.ppermute(w_sum, "c", swap)
    w_part = w_sum
    w_part, relay, straight = lax.optimization_barrier((w_part, relay, straight))
    for m in range(1, 4):
        w_sum = w_sum + lax.ppermute(w_part, "zh", [(i, i ^ m) for i in range(ZH)])
    w_part = w_sum
    relayed = lax.ppermute((aside + relayed).astype(bf16), ("y", "c"), ahead).astype(f32)
    for m in range(1, 4):
        w_sum = w_sum + lax.ppermute(w_part, "y", [(i, (i + m) % Y) for i in range(Y)])
    chunks = (keep + direct + relayed).reshape(4, share, width)
    grad = lax.dynamic_index_in_dim(chunks, zh, 0, False)
    for m in range(1, 4):
        chunk = lax.dynamic_index_in_dim(chunks, zh ^ m, 0, False).astype(bf16)
        grad = grad + lax.ppermute(chunk, "zh", [(i, i ^ m) for i in range(ZH)]).astype(f32)
    feature_grad = (chunk_deg * grad).astype(bf16)
    weight_grad = lax.all_to_all(jnp.broadcast_to(w_sum[None], (reps,) + w_sum.shape), REP, 0, 0)
    return (activated, weight_grad.reshape(width, width), feature_grad)


def solution(mesh):
    fine = Mesh(mesh.devices.reshape(ZH, Y, C, ZL, X), ALL)
    placed = (
        P(ROWS, None),
        P(ROWS),
        P(),
        P(ROWS, REP, None, None),
        P(ROWS, REP),
        P(ROWS, REP),
        P(ROWS, REP),
        P(ROWS, None),
    )
    return jax.shard_map(
        shards,
        mesh=fine,
        in_specs=placed,
        out_specs=(P(ALL, None), P(), P(REP + ROWS, None)),
        check_vma=False,
    )
```

```python
import jax
import jax.numpy as jnp
from jax import lax
from jax.experimental import pallas as pl
from jax.experimental.pallas import tpu as pltpu
from jax.sharding import Mesh, PartitionSpec as P

ZH, Y, C, ZL, X = 4, 4, 2, 2, 4
ROWS = ("zh", "y", "c")
REP = ("zl", "x")
ALL = ROWS + REP
TILE = 128
PIECE = 4 * TILE
WROWS = 64
BF16, F32 = jnp.bfloat16, jnp.float32
SMEM = pl.BlockSpec(memory_space=pltpu.SMEM)
WHOLE = pl.BlockSpec(memory_space=pltpu.VMEM)
HBM = pl.BlockSpec(memory_space=pltpu.HBM)


def flat(zh, y, c, zl, x):
    return (((zh * Y + y) * C + c) * ZL + zl) * X + x


def place_of(q, r):
    return (2 * (r % 2) + q // 2 + (q % 2) * (2 * (q // 2) - 1)) % Y


def piece_route():
    pairs = []
    for j in range(ZH * Y * C):
        for k in range(ZL * X):
            r = j // 4
            dx = (k % X - r % X) % X
            if k // X == r // X:
                near, far = 0, 3 if r // X == 0 else 1
            else:
                near, far = 1 if r // X == 0 else 3, 2
            zh = (j // (Y * C) + (far if dx < 2 else near)) % ZH
            pairs.append((j * (ZL * X) + k, flat(zh, place_of(j % 4, r), dx % 2, r // X, r % X)))
    return pairs


def ring_route(back):
    pairs = []
    for y in range(Y):
        for c in range(C):
            step = 1 if (c == 0) != back else -1
            pairs.append((y * C + c, (y + step) % Y * C + c))
    return pairs


def order_of(apart, parity):
    return jnp.where((apart & 1) == 0, 3 * (apart >> 1), 1 + (((3 - apart) >> 1) ^ parity))


def apart_of(q, odd, y):
    high, low = q >> 1, q & 1
    return (2 * odd + high + low * (2 * high - 1) - y) & 3


def down(row):
    square = jnp.transpose(jnp.broadcast_to(row, (TILE, TILE)))
    return jnp.concatenate([square, square], 1)


def call(body, name, outs, scalars, arrays, specs=None, scratch=(), limit=16):
    return pl.pallas_call(
        body,
        out_shape=outs,
        in_specs=[SMEM] * len(scalars) + (specs or [WHOLE] * len(arrays)),
        out_specs=jax.tree.map(lambda _: WHOLE, outs),
        scratch_shapes=list(scratch),
        compiler_params=pltpu.CompilerParams(vmem_limit_bytes=limit << 20),
        name=name,
    )(*scalars, *arrays)


def piece_body(half, degrees, features, out, tiles, sems):
    def copy(k):
        at = pl.ds(pl.multiple_of((2 * k + half[0]) * TILE, TILE), TILE)
        return pltpu.make_async_copy(features.at[at], tiles.at[k], sems.at[k])

    for k in range(4):
        copy(k).start()
    all_rows = degrees[...].astype(F32)
    line = lax.broadcasted_iota(jnp.int32, (16, TILE), 0)
    below = jnp.zeros((16, TILE), F32)
    columns = []
    for k in range(4):
        row = jnp.where(half[0] == 0, all_rows[2 * k : 2 * k + 1], all_rows[2 * k + 1 : 2 * k + 2])
        below = jnp.where(line == k, jnp.broadcast_to(row, (16, TILE)), below)
        columns.append(down(row))
    out[PIECE : PIECE + 16, :] = jnp.concatenate([below, below], 1).astype(BF16)
    for k in range(4):
        copy(k).wait()
        out[k * TILE : (k + 1) * TILE, :] = (columns[k] * tiles[k].astype(F32)).astype(BF16)


def share_body(replica, degrees, features, cotangent, scaled, cot, deg, tile, sems):
    at = pl.ds(pl.multiple_of(replica[0] * TILE, TILE), TILE)
    first = pltpu.make_async_copy(features.at[at], tile, sems.at[0])
    second = pltpu.make_async_copy(cotangent.at[at], cot, sems.at[1])
    first.start()
    second.start()
    line = lax.broadcasted_iota(jnp.int32, (8, TILE), 0)
    row = jnp.sum(jnp.where(line == replica[0], degrees[...].astype(F32), 0.0), 0, keepdims=True)
    column = down(row)
    deg[...] = column
    first.wait()
    scaled[...] = (column * tile[...].astype(F32)).astype(BF16)
    second.wait()


def assemble_body(count, core, y, odd, row, col, vals, own, other, dense, sems, out_sems):
    dense[...] = jnp.zeros_like(dense)
    total = count[0, 0] + count[0, 1] + count[0, 2] + count[0, 3]

    @pl.loop(0, total)
    def _(k):
        at = col[0, k]
        q, sub = at >> 3, at & 7
        parity, pair = sub & 1, sub >> 1
        place = (parity ^ core[0]) * 16 + order_of(apart_of(q, odd[0], y[0]), parity) * 4 + pair
        rows = pl.ds(pl.multiple_of(row[0, k] * TILE, TILE), TILE)
        cols = pl.ds(pl.multiple_of(place * TILE, TILE), TILE)
        pltpu.make_async_copy(vals.at[0, k], dense.at[rows, cols], sems.at[k]).start()

    @pl.loop(0, total)
    def _(k):
        corner = (pl.ds(0, TILE), pl.ds(0, TILE))
        pltpu.make_async_copy(vals.at[0, k], dense.at[corner], sems.at[k]).wait()

    width = own.shape[1]
    halves = [
        pltpu.make_async_copy(dense.at[:, pl.ds(i * width, width)], out, out_sems.at[i])
        for i, out in enumerate((own, other))
    ]
    for half in halves:
        half.start()
    for half in halves:
        half.wait()


def assemble(count, ids, row, col, vals, rows, cols):
    half = jax.ShapeDtypeStruct((rows, cols), BF16)
    return pl.pallas_call(
        assemble_body,
        out_shape=(half, half),
        in_specs=[SMEM] * 6 + [HBM],
        out_specs=(HBM, HBM),
        scratch_shapes=[
            pltpu.VMEM((rows, 2 * cols), BF16),
            pltpu.SemaphoreType.DMA((vals.shape[1],)),
            pltpu.SemaphoreType.DMA((2,)),
        ],
        name="assemble",
    )(count, *ids, row, col, vals)


def middle_body(factor, parts, scaled, cot, deg, weight, activated, both):
    summed = parts[0].astype(F32)
    for s in range(1, ZL * X):
        summed += parts[s].astype(F32)
    column = deg[...]
    propagated = (column * (summed + scaled[...].astype(F32))).astype(BF16)
    preact = jnp.dot(propagated, weight[...], preferred_element_type=F32)
    gate = jax.nn.sigmoid(preact)
    activated[...] = (preact * gate).astype(BF16)
    grad_pre = (cot[...].astype(F32) * gate * (1.0 + preact * (1.0 - gate))).astype(BF16)
    back = lax.dot_general(grad_pre, weight[...], (((1,), (1,)), ((), ())), preferred_element_type=F32)
    back = (column * back).astype(BF16)
    grad = lax.dot_general(propagated, grad_pre, (((0,), (0,)), ((), ())), preferred_element_type=F32)
    grad = (grad * factor).astype(BF16)
    for s in range(ZL * X):
        part = s // X * 2 + s % 2
        both[s, :TILE, :] = back
        both[s, TILE:, :] = grad[part * WROWS : (part + 1) * WROWS]


def regroup(ids, parity, rows, both, outs, others):
    y, odd, owner, q_own = ids
    for i, out in enumerate(outs):
        pair = (y + (0, 3 - 2 * parity, 1 + 2 * parity, 2)[i]) & 3

        def load(q, at):
            place = order_of(apart_of(q, odd, y), parity) * 4 + pair
            part = rows[pl.ds(pl.multiple_of(place * TILE, TILE), TILE), :]
            if others is None:
                return part
            return part + others[pl.ds(pl.multiple_of(i * PIECE + at, TILE), TILE), :].astype(F32)

        for q in range(4):
            out[q * TILE : (q + 1) * TILE, :] = load(q, q * TILE).astype(out.dtype)

        @pl.when(owner != 0)
        def _():
            at = pl.multiple_of(q_own * TILE, TILE)
            mine = load(q_own, at) + both[2 * pair + parity, :TILE, :].astype(F32)
            out[pl.ds(at, TILE), :] = mine.astype(out.dtype)


def slice_sum(both):
    total = both[0, TILE:, :].astype(F32)
    for s in range(1, ZL * X):
        total += both[s, TILE:, :].astype(F32)
    return total.astype(BF16)


def send_body(core, y, odd, owner, q_own, rows, both, out):
    outs = [out.at[i * PIECE : (i + 1) * PIECE] for i in range(4)]
    regroup((y[0], odd[0], owner[0], q_own[0]), 1 - core[0], rows, both, outs, None)
    out[4 * PIECE :, :] = slice_sum(both)


def keep_body(core, y, odd, owner, q_own, rows, both, others, keep, straight, aside, relay, w_own):
    outs = (keep, straight.at[:PIECE], aside, relay.at[:PIECE])
    regroup((y[0], odd[0], owner[0], q_own[0]), core[0], rows, both, outs, others)
    w_rows = (slice_sum(both).astype(F32) + others[4 * PIECE :, :].astype(F32)).astype(BF16)
    straight[PIECE:, :] = w_rows
    relay[PIECE:, :] = w_rows
    w_own[...] = w_rows


def relay_body(aside, came, out):
    out[:PIECE, :] = (aside[...] + came[:PIECE, :].astype(F32)).astype(BF16)
    out[PIECE:, :] = came[PIECE:, :]


def spread_body(zh, keep, direct, relayed, first, w_own, own, out1, out2, out3, w_out):
    w_rows = w_own[...].astype(F32) + first[PIECE:, :].astype(F32)
    w_rows = (w_rows + (direct[PIECE:, :].astype(F32) + relayed[PIECE:, :].astype(F32))).astype(BF16)
    w_out[...] = w_rows
    for m, out in enumerate((own, out1, out2, out3)):
        at = pl.ds(pl.multiple_of((zh[0] ^ m) * TILE, TILE), TILE)
        chunk = keep[at, :] + direct[at, :].astype(F32) + relayed[at, :].astype(F32)
        out[:TILE, :] = chunk.astype(out.dtype)
        if m:
            out[TILE:, :] = w_rows


def last_body(core, y, odd, zh, own, came1, came2, came3, w_rows, p0, p1, p2, p3, grad, w_out):
    order = order_of(apart_of(zh[0], odd[0], y[0]), core[0])
    below = jnp.zeros((16, TILE), F32)
    for i, piece in enumerate((p0, p1, p2, p3)):
        below = jnp.where(order == i, piece[PIECE:, :TILE].astype(F32), below)
    line = lax.broadcasted_iota(jnp.int32, (16, TILE), 0)
    row = jnp.sum(jnp.where(line == y[0], below, 0.0), 0, keepdims=True)
    total = own[...]
    w_sum = w_rows[...].astype(F32)
    for came in (came1, came2, came3):
        total += came[:TILE, :].astype(F32)
        w_sum += came[TILE:, :].astype(F32)
    grad[...] = (down(row) * total).astype(BF16)
    w_out[...] = w_sum


def join_body(zl, xl, mine, over_z, over_x, over_both, out):
    for part, flip_z, flip_x in ((mine, 0, 0), (over_z, 1, 0), (over_x, 0, 1), (over_both, 1, 1)):
        at = ((zl[0] ^ flip_z) * 2 + (xl[0] ^ flip_x)) * WROWS
        out[pl.ds(pl.multiple_of(at, WROWS), WROWS), :] = part[...]


def shards(features, inv_sqrt_degree, weight, tile_vals, tile_row, tile_col, tile_count, cotangent):
    nodes_block, width = features.shape
    zh, y, core, zl, x = (lax.axis_index(a).reshape(1) for a in ALL)
    replica, block = lax.axis_index(REP), lax.axis_index(ROWS)
    nodes = nodes_block * ZH * Y * C
    cols = Y * PIECE
    odd = x & 1
    degrees = inv_sqrt_degree.reshape(nodes_block // TILE, TILE)

    def held(rows, kind=BF16):
        return pltpu.VMEM((rows, width), kind)

    piece = call(
        piece_body, "piece", held(PIECE + 16), [(x + (y >> 1)) & 1], [degrees, features], [WHOLE, HBM],
        [pltpu.VMEM((4, TILE, width), BF16), pltpu.SemaphoreType.DMA((4,))],
    )
    piece = lax.ppermute(piece, ALL, piece_route())
    scaled, cot, deg = call(
        share_body, "share", (held(TILE), held(TILE), held(TILE, F32)), [replica.reshape(1)],
        [degrees, features, cotangent], [WHOLE, HBM, HBM],
        [pltpu.VMEM((TILE, width), BF16), pltpu.SemaphoreType.DMA((2,))],
    )
    own_a, other_a = assemble(tile_count, [core, y, odd], tile_row, tile_col, tile_vals, nodes_block, cols)
    piece, own_a, other_a = lax.optimization_barrier((piece, own_a, other_a))

    swap = [(0, 1), (1, 0)]
    ahead, behind = ring_route(False), ring_route(True)
    first = lax.ppermute(piece, ("y", "c"), ahead)
    second = lax.ppermute(piece, ("y", "c"), behind)
    third = lax.ppermute(first, ("y", "c"), ahead)
    pieces = [piece, first, second, third]
    partial = jnp.zeros((nodes_block, width), F32)
    for i, own_x in enumerate(pieces):
        other_x = lax.ppermute(own_x, "c", swap)
        at = slice(i * PIECE, (i + 1) * PIECE)
        partial = partial + jnp.dot(own_a[:, at], own_x[:PIECE], preferred_element_type=F32)
        partial = partial + jnp.dot(other_a[:, at], other_x[:PIECE], preferred_element_type=F32)
    partial, scaled, cot, deg = lax.optimization_barrier((partial.astype(BF16), scaled, cot, deg))
    parts = lax.all_to_all(partial.reshape(ZL * X, TILE, width), REP, 0, 0)
    activated, both = call(
        lambda *refs: middle_body(float(nodes) ** -0.5, *refs),
        "middle",
        (jax.ShapeDtypeStruct((TILE, width), BF16), pltpu.VMEM((ZL * X, TILE + WROWS, width), BF16)),
        [],
        [parts, scaled, cot, deg, weight],
    )
    both = lax.all_to_all(both, REP, 0, 0)
    back_block = both[:, :TILE].reshape(nodes_block, width)
    ids = [core, y, odd, (replica == block // 4).astype(jnp.int32).reshape(1), (block % 4).reshape(1)]

    def pull(a):
        return lax.dot_general(a, back_block, (((0,), (0,)), ((), ())), preferred_element_type=F32)

    others = call(send_body, "regroup_send", held(cols + WROWS), ids, [pull(other_a), both])
    others = lax.ppermute(others, "c", swap)
    keep, straight, aside, relay, w_own = call(
        keep_body,
        "regroup_keep",
        (held(PIECE, F32), held(PIECE + WROWS), held(PIECE, F32), held(PIECE + WROWS), held(WROWS)),
        ids,
        [pull(own_a), both, others],
    )
    came = lax.ppermute(relay, ("y", "c"), ahead)
    direct = lax.ppermute(straight, ("y", "c"), behind)
    relayed = call(relay_body, "relay", held(PIECE + WROWS), [], [aside, came])
    relayed = lax.ppermute(relayed, ("y", "c"), ahead)
    own, *sent, w_rows = call(
        spread_body,
        "spread",
        (held(TILE, F32), held(TILE + WROWS), held(TILE + WROWS), held(TILE + WROWS), held(WROWS)),
        [zh],
        [keep, direct, relayed, came, w_own],
    )
    got = [lax.ppermute(sent[m - 1], "zh", [(i, i ^ m) for i in range(ZH)]) for m in range(1, 4)]
    feature_grad, w_mine = call(
        last_body,
        "last",
        (jax.ShapeDtypeStruct((TILE, width), BF16), held(WROWS, F32)),
        [core, y, odd, zh],
        [own, *got, w_rows, *pieces],
    )
    flip = [(i, i ^ 1) for i in range(X)]
    over_z = lax.ppermute(w_mine, "zl", swap)
    over_x = lax.ppermute(w_mine, "x", flip)
    over_both = lax.ppermute(over_z, "x", flip)
    weight_grad = call(
        join_body,
        "join",
        jax.ShapeDtypeStruct((width, width), F32),
        [zl, x & 1],
        [w_mine, over_z, over_x, over_both],
    )
    return (activated, weight_grad, feature_grad)


def solution(mesh):
    fine = Mesh(mesh.devices.reshape(ZH, Y, C, ZL, X), ALL)
    placed = (
        P(ROWS, None),
        P(ROWS),
        P(),
        P(ROWS, REP, None, None),
        P(ROWS, REP),
        P(ROWS, REP),
        P(ROWS, REP),
        P(ROWS, None),
    )
    return jax.shard_map(
        shards,
        mesh=fine,
        in_specs=placed,
        out_specs=(P(ALL, None), P(), P(REP + ROWS, None)),
        check_vma=False,
    )
```

```python
import jax
import jax.numpy as jnp
from jax import lax
from jax.experimental import pallas as pl
from jax.experimental.pallas import tpu as pltpu
from jax.sharding import Mesh, PartitionSpec as P

ZH, Y, C, ZL, X = 4, 4, 2, 2, 4
ROWS = ("zh", "y", "c")
REP = ("zl", "x")
ALL = ROWS + REP
TILE = 128
PIECE = 4 * TILE
HALF = 2 * TILE
WROWS = 64
LIMIT = None
BF16, F32 = jnp.bfloat16, jnp.float32
SMEM = pl.BlockSpec(memory_space=pltpu.SMEM)
WHOLE = pl.BlockSpec(memory_space=pltpu.VMEM)
HBM = pl.BlockSpec(memory_space=pltpu.HBM)


def flat(zh, y, c, zl, x):
    return (((zh * Y + y) * C + c) * ZL + zl) * X + x


def place_of(q, r):
    return (2 * (r % 2) + q // 2 + (q % 2) * (2 * (q // 2) - 1)) % Y


def piece_route():
    pairs = []
    for j in range(ZH * Y * C):
        for k in range(ZL * X):
            r = j // 4
            dx = (k % X - r % X) % X
            if k // X == r // X:
                near, far = 0, 3 if r // X == 0 else 1
            else:
                near, far = 1 if r // X == 0 else 3, 2
            zh = (j // (Y * C) + (far if dx < 2 else near)) % ZH
            pairs.append((j * (ZL * X) + k, flat(zh, place_of(j % 4, r), dx % 2, r // X, r % X)))
    return pairs


def ring_route(step):
    return [(y, (y + step) % Y) for y in range(Y)]


def order_of(apart):
    return jnp.where((apart & 1) == 0, 3 * (apart >> 1), 1 + ((3 - apart) >> 1))


def apart_of(q, odd, y):
    high, low = q >> 1, q & 1
    return (2 * odd + high + low * (2 * high - 1) - y) & 3


def down(row):
    square = jnp.transpose(jnp.broadcast_to(row, (TILE, TILE)))
    return jnp.concatenate([square, square], 1)


def call(body, name, outs, scalars, arrays, specs=None, scratch=(), limit=16 << 20):
    return pl.pallas_call(
        body,
        out_shape=outs,
        in_specs=[SMEM] * len(scalars) + (specs or [WHOLE] * len(arrays)),
        out_specs=jax.tree.map(lambda _: WHOLE, outs),
        scratch_shapes=list(scratch),
        compiler_params=pltpu.CompilerParams(vmem_limit_bytes=limit),
        name=name,
    )(*scalars, *arrays)


def piece_body(half, degrees, features, out, tiles, sems):
    def copy(k):
        at = pl.ds(pl.multiple_of((2 * k + half[0]) * TILE, TILE), TILE)
        return pltpu.make_async_copy(features.at[at], tiles.at[k], sems.at[k])

    for k in range(4):
        copy(k).start()
    all_rows = degrees[...].astype(F32)
    line = lax.broadcasted_iota(jnp.int32, (16, TILE), 0)
    below = jnp.zeros((16, TILE), F32)
    columns = []
    for k in range(4):
        row = jnp.where(half[0] == 0, all_rows[2 * k : 2 * k + 1], all_rows[2 * k + 1 : 2 * k + 2])
        below = jnp.where(line == k, jnp.broadcast_to(row, (16, TILE)), below)
        columns.append(down(row))
    out[PIECE : PIECE + 16, :] = jnp.concatenate([below, below], 1).astype(BF16)
    for k in range(4):
        copy(k).wait()
        out[k * TILE : (k + 1) * TILE, :] = (columns[k] * tiles[k].astype(F32)).astype(BF16)


def share_body(replica, degrees, features, cotangent, scaled, cot, deg, tile, sems):
    at = pl.ds(pl.multiple_of(replica[0] * TILE, TILE), TILE)
    first = pltpu.make_async_copy(features.at[at], tile, sems.at[0])
    second = pltpu.make_async_copy(cotangent.at[at], cot, sems.at[1])
    first.start()
    second.start()
    line = lax.broadcasted_iota(jnp.int32, (8, TILE), 0)
    row = jnp.sum(jnp.where(line == replica[0], degrees[...].astype(F32), 0.0), 0, keepdims=True)
    column = down(row)
    deg[...] = column
    first.wait()
    scaled[...] = (column * tile[...].astype(F32)).astype(BF16)
    second.wait()


def assemble_body(count, core, y, odd, row, col, vals, own, other, dense, sems, out_sems):
    dense[...] = jnp.zeros_like(dense)
    total = count[0, 0] + count[0, 1] + count[0, 2] + count[0, 3]

    @pl.loop(0, total)
    def _(k):
        at = col[0, k]
        q, sub = at >> 3, at & 7
        parity, pair = sub & 1, sub >> 1
        place = (parity ^ core[0]) * 16 + order_of(apart_of(q, odd[0], y[0])) * 4 + pair
        rows = pl.ds(pl.multiple_of(row[0, k] * TILE, TILE), TILE)
        cols = pl.ds(pl.multiple_of(place * TILE, TILE), TILE)
        pltpu.make_async_copy(vals.at[0, k], dense.at[rows, cols], sems.at[k]).start()

    @pl.loop(0, total)
    def _(k):
        corner = (pl.ds(0, TILE), pl.ds(0, TILE))
        pltpu.make_async_copy(vals.at[0, k], dense.at[corner], sems.at[k]).wait()

    width = own.shape[1]
    halves = [
        pltpu.make_async_copy(dense.at[:, pl.ds(i * width, width)], out, out_sems.at[i])
        for i, out in enumerate((own, other))
    ]
    for half in halves:
        half.start()
    for half in halves:
        half.wait()


def assemble(count, ids, row, col, vals, rows, cols):
    half = jax.ShapeDtypeStruct((rows, cols), BF16)
    return pl.pallas_call(
        assemble_body,
        out_shape=(half, half),
        in_specs=[SMEM] * 6 + [HBM],
        out_specs=(HBM, HBM),
        scratch_shapes=[
            pltpu.VMEM((rows, 2 * cols), BF16),
            pltpu.SemaphoreType.DMA((vals.shape[1],)),
            pltpu.SemaphoreType.DMA((2,)),
        ],
        name="assemble",
    )(count, *ids, row, col, vals)


def middle_body(factor, parts, scaled, cot, deg, weight, activated, both):
    summed = parts[0].astype(F32)
    for s in range(1, ZL * X):
        summed += parts[s].astype(F32)
    column = deg[...]
    propagated = (column * (summed + scaled[...].astype(F32))).astype(BF16)
    preact = jnp.dot(propagated, weight[...], preferred_element_type=F32)
    gate = jax.nn.sigmoid(preact)
    activated[...] = (preact * gate).astype(BF16)
    grad_pre = (cot[...].astype(F32) * gate * (1.0 + preact * (1.0 - gate))).astype(BF16)
    back = lax.dot_general(grad_pre, weight[...], (((1,), (1,)), ((), ())), preferred_element_type=F32)
    back = (column * back).astype(BF16)
    grad = lax.dot_general(propagated, grad_pre, (((0,), (0,)), ((), ())), preferred_element_type=F32)
    grad = (grad * factor).astype(BF16)
    for s in range(ZL * X):
        part = s // X * 2 + s % 2
        both[s, :TILE, :] = back
        both[s, TILE:, :] = grad[part * WROWS : (part + 1) * WROWS]


def regroup(ids, parity, rows, both, outs, others):
    y, odd, owner, q_own = ids
    for i, out in enumerate(outs):
        pair = (y + (0, 3, 1, 2)[i]) & 3

        def load(q, at):
            place = order_of(apart_of(q, odd, y)) * 4 + pair
            part = rows[pl.ds(pl.multiple_of(place * TILE, TILE), TILE), :]
            if others is None:
                return part
            return part + others[pl.ds(pl.multiple_of(i * PIECE + at, TILE), TILE), :].astype(F32)

        for q in range(4):
            out[q * TILE : (q + 1) * TILE, :] = load(q, q * TILE).astype(out.dtype)

        @pl.when(owner != 0)
        def _():
            at = pl.multiple_of(q_own * TILE, TILE)
            mine = load(q_own, at) + both[2 * pair + parity, :TILE, :].astype(F32)
            out[pl.ds(at, TILE), :] = mine.astype(out.dtype)


def slice_sum(both):
    total = both[0, TILE:, :].astype(F32)
    for s in range(1, ZL * X):
        total += both[s, TILE:, :].astype(F32)
    return total.astype(BF16)


def send_body(core, y, odd, owner, q_own, rows, both, out):
    outs = [out.at[i * PIECE : (i + 1) * PIECE] for i in range(4)]
    regroup((y[0], odd[0], owner[0], q_own[0]), 1 - core[0], rows, both, outs, None)
    out[4 * PIECE :, :] = slice_sum(both)


def keep_body(core, y, odd, owner, q_own, rows, both, others, keep, behind, ahead, up, down_, w_own, far):
    regroup((y[0], odd[0], owner[0], q_own[0]), core[0], rows, both, (keep, behind, ahead, far), others)
    for i, out in enumerate((up, down_)):
        out[...] = far[i * HALF : (i + 1) * HALF, :]
    w_own[...] = (slice_sum(both).astype(F32) + others[4 * PIECE :, :].astype(F32)).astype(BF16)


def relay_body(behind, ahead, up, down_, mine, came1, came2, came3, up_out, down_out, w_out):
    for i, (rows, came, out) in enumerate(((ahead, up, up_out), (behind, down_, down_out))):
        for k in range(2):
            part = slice(k * HALF, (k + 1) * HALF)
            value = rows[part, :]
            if k == i:
                value += came[...].astype(F32)
            out[part, :] = value.astype(BF16)
    total = mine[...].astype(F32) + came1[...].astype(F32)
    w_out[...] = total + (came2[...].astype(F32) + came3[...].astype(F32))


def spread_body(zh, keep, up2, down2, own, out1, out2, out3):
    for m, out in enumerate((own, out1, out2, out3)):
        at = pl.ds(pl.multiple_of((zh[0] ^ m) * TILE, TILE), TILE)
        chunk = keep[at, :] + up2[at, :].astype(F32) + down2[at, :].astype(F32)
        out[...] = chunk.astype(out.dtype)


def pass_body(source, out):
    out[...] = source[...]


def add_body(mine, came1, came2, came3, after, out):
    total = mine[...].astype(F32) + came1[...].astype(F32)
    out[...] = total + (came2[...].astype(F32) + came3[...].astype(F32))


def last_body(y, odd, zh, own, came1, came2, came3, p0, p1, p2, p3, grad):
    order = order_of(apart_of(zh[0], odd[0], y[0]))
    below = jnp.zeros((16, TILE), F32)
    for i, piece in enumerate((p0, p1, p2, p3)):
        below = jnp.where(order == i, piece[piece.shape[0] - 16 :, :TILE].astype(F32), below)
    line = lax.broadcasted_iota(jnp.int32, (16, TILE), 0)
    row = jnp.sum(jnp.where(line == y[0], below, 0.0), 0, keepdims=True)
    total = own[...]
    for came in (came1, came2, came3):
        total += came[...].astype(F32)
    grad[...] = (down(row) * total).astype(BF16)


def join_body(zl, xl, mine, over_z, over_x, over_both, out):
    for part, flip_z, flip_x in ((mine, 0, 0), (over_z, 1, 0), (over_x, 0, 1), (over_both, 1, 1)):
        at = ((zl[0] ^ flip_z) * 2 + (xl[0] ^ flip_x)) * WROWS
        out[pl.ds(pl.multiple_of(at, WROWS), WROWS), :] = part[...]


def shards(features, inv_sqrt_degree, weight, tile_vals, tile_row, tile_col, tile_count, cotangent):
    nodes_block, width = features.shape
    zh, y, core, zl, x = (lax.axis_index(a).reshape(1) for a in ALL)
    replica, block = lax.axis_index(REP), lax.axis_index(ROWS)
    nodes = nodes_block * ZH * Y * C
    cols = Y * PIECE
    odd = x & 1
    degrees = inv_sqrt_degree.reshape(nodes_block // TILE, TILE)

    def held(rows, kind=BF16):
        return pltpu.VMEM((rows, width), kind)

    piece = call(
        piece_body, "piece", held(PIECE + 16), [(x + (y >> 1)) & 1], [degrees, features], [WHOLE, HBM],
        [pltpu.VMEM((4, TILE, width), BF16), pltpu.SemaphoreType.DMA((4,))], LIMIT,
    )
    piece = lax.ppermute(piece, ALL, piece_route())
    scaled, cot, deg = call(
        share_body, "share", (held(TILE), held(TILE), held(TILE, F32)), [replica.reshape(1)],
        [degrees, features, cotangent], [WHOLE, HBM, HBM],
        [pltpu.VMEM((TILE, width), BF16), pltpu.SemaphoreType.DMA((2,))], LIMIT,
    )
    own_a, other_a = assemble(tile_count, [core, y, odd], tile_row, tile_col, tile_vals, nodes_block, cols)
    piece, own_a, other_a = lax.optimization_barrier((piece, own_a, other_a))

    swap = [(0, 1), (1, 0)]
    ahead, behind = ring_route(1), ring_route(-1)
    partial = jnp.dot(own_a[:, :PIECE], piece[:PIECE], preferred_element_type=F32)
    first = lax.ppermute(piece, "y", ahead)
    second = lax.ppermute(piece, "y", behind)
    third = lax.ppermute(first[:HALF], "y", ahead)
    fourth = lax.ppermute(second[HALF:], "y", behind)
    pieces = [piece, first, second, fourth]
    at = 0
    for own_x in (piece, first, second, third, fourth):
        other_x = lax.ppermute(own_x, "c", swap)
        size = own_x.shape[0] // TILE * TILE
        if at:
            partial = partial + jnp.dot(own_a[:, at : at + size], own_x[:size], preferred_element_type=F32)
        partial = partial + jnp.dot(other_a[:, at : at + size], other_x[:size], preferred_element_type=F32)
        at += size
    partial = partial.astype(BF16)
    partial, scaled, cot, deg = lax.optimization_barrier((partial, scaled, cot, deg))
    parts = lax.all_to_all(partial.reshape(ZL * X, TILE, width), REP, 0, 0)
    activated, both = call(
        lambda *refs: middle_body(float(nodes) ** -0.5, *refs),
        "middle",
        (jax.ShapeDtypeStruct((TILE, width), BF16), pltpu.VMEM((ZL * X, TILE + WROWS, width), BF16)),
        [],
        [parts, scaled, cot, deg, weight],
    )
    both = lax.all_to_all(both, REP, 0, 0)
    back_block = both[:, :TILE].reshape(nodes_block, width)
    ids = [core, y, odd, (replica == block // 4).astype(jnp.int32).reshape(1), (block % 4).reshape(1)]

    def pull(a):
        return lax.dot_general(a, back_block, (((0,), (0,)), ((), ())), preferred_element_type=F32)

    others = call(send_body, "regroup_send", held(cols + WROWS), ids, [pull(other_a), both])
    others = lax.ppermute(others, "c", swap)
    keep, behind_rows, ahead_rows, up, down_, w_own = call(
        keep_body,
        "regroup_keep",
        (held(PIECE, F32), held(PIECE, F32), held(PIECE, F32), held(HALF), held(HALF), held(WROWS)),
        ids,
        [pull(own_a), both, others],
        scratch=[held(PIECE)],
    )
    up, down_ = lax.ppermute(up, "y", ahead), lax.ppermute(down_, "y", behind)
    w_rows = call(pass_body, "slices", held(WROWS), [], [w_own])
    w_y = [lax.ppermute(w_rows, "y", ring_route(m)) for m in range(1, 4)]
    up2, down2, w_rows = call(
        relay_body,
        "relay",
        (held(PIECE), held(PIECE), held(WROWS, F32)),
        [],
        [behind_rows, ahead_rows, up, down_, w_rows, *w_y],
    )
    up2, down2 = lax.ppermute(up2, "y", ahead), lax.ppermute(down2, "y", behind)
    w_rows = call(pass_body, "slices_y", held(WROWS, F32), [], [w_rows])
    exchange = [[(i, i ^ m) for i in range(ZH)] for m in range(1, 4)]
    w_z = [lax.ppermute(w_rows, "zh", route) for route in exchange]
    own, *sent = call(
        spread_body,
        "spread",
        (held(TILE, F32), held(TILE), held(TILE), held(TILE)),
        [zh],
        [keep, up2, down2],
    )
    w_mine = call(add_body, "slices_z", held(WROWS, F32), [], [w_rows, *w_z, sent[0]])
    got = [lax.ppermute(part, "zh", route) for part, route in zip(sent, exchange)]
    feature_grad = call(
        last_body,
        "last",
        jax.ShapeDtypeStruct((TILE, width), BF16),
        [y, odd, zh],
        [own, *got, *pieces],
    )
    flip = [(i, i ^ 1) for i in range(X)]
    over_z = lax.ppermute(w_mine, "zl", swap)
    over_x = lax.ppermute(w_mine, "x", flip)
    over_both = lax.ppermute(w_mine, REP, [(i, i ^ 5) for i in range(ZL * X)])
    weight_grad = call(
        join_body,
        "join",
        jax.ShapeDtypeStruct((width, width), F32),
        [zl, x & 1],
        [w_mine, over_z, over_x, over_both],
    )
    return (activated, weight_grad, feature_grad)


def solution(mesh):
    fine = Mesh(mesh.devices.reshape(ZH, Y, C, ZL, X), ALL)
    placed = (
        P(ROWS, None),
        P(ROWS),
        P(),
        P(ROWS, REP, None, None),
        P(ROWS, REP),
        P(ROWS, REP),
        P(ROWS, REP),
        P(ROWS, None),
    )
    return jax.shard_map(
        shards,
        mesh=fine,
        in_specs=placed,
        out_specs=(P(ALL, None), P(), P(REP + ROWS, None)),
        check_vma=False,
    )
```

```python
import jax
import jax.numpy as jnp
from jax import lax
from jax.experimental import pallas as pl
from jax.experimental.pallas import tpu as pltpu
from jax.sharding import Mesh, PartitionSpec as P

ZH, Y, C, ZL, X = 4, 4, 2, 2, 4
ROWS = ("zh", "y", "c")
REP = ("zl", "x")
ALL = ROWS + REP
TILE = 128
PIECE = 4 * TILE
HALF = 2 * TILE
WROWS = 64
LIMIT = None
BF16, F32 = jnp.bfloat16, jnp.float32
SMEM = pl.BlockSpec(memory_space=pltpu.SMEM)
WHOLE = pl.BlockSpec(memory_space=pltpu.VMEM)
HBM = pl.BlockSpec(memory_space=pltpu.HBM)


def flat(zh, y, c, zl, x):
    return (((zh * Y + y) * C + c) * ZL + zl) * X + x


def place_of(q, r):
    return (2 * (r % 2) + q // 2 + (q % 2) * (2 * (q // 2) - 1)) % Y


def piece_route():
    pairs = []
    for j in range(ZH * Y * C):
        for k in range(ZL * X):
            r = j // 4
            dx = (k % X - r % X) % X
            if k // X == r // X:
                near, far = 0, 3 if r // X == 0 else 1
            else:
                near, far = 1 if r // X == 0 else 3, 2
            zh = (j // (Y * C) + (far if dx < 2 else near)) % ZH
            pairs.append((j * (ZL * X) + k, flat(zh, place_of(j % 4, r), dx % 2, r // X, r % X)))
    return pairs


def ring_route(step):
    return [(y, (y + step) % Y) for y in range(Y)]


def order_of(apart):
    return jnp.where((apart & 1) == 0, 3 * (apart >> 1), 1 + ((3 - apart) >> 1))


def apart_of(q, odd, y):
    high, low = q >> 1, q & 1
    return (2 * odd + high + low * (2 * high - 1) - y) & 3


def down(row):
    square = jnp.transpose(jnp.broadcast_to(row, (TILE, TILE)))
    return jnp.concatenate([square, square], 1)


def call(body, name, outs, scalars, arrays, specs=None, scratch=(), limit=16 << 20):
    return pl.pallas_call(
        body,
        out_shape=outs,
        in_specs=[SMEM] * len(scalars) + (specs or [WHOLE] * len(arrays)),
        out_specs=jax.tree.map(lambda _: WHOLE, outs),
        scratch_shapes=list(scratch),
        compiler_params=pltpu.CompilerParams(vmem_limit_bytes=limit),
        name=name,
    )(*scalars, *arrays)


def piece_body(half, degrees, features, out, tiles, sems):
    def copy(k):
        at = pl.ds(pl.multiple_of((2 * k + half[0]) * TILE, TILE), TILE)
        return pltpu.make_async_copy(features.at[at], tiles.at[k], sems.at[k])

    for k in range(4):
        copy(k).start()
    all_rows = degrees[...].astype(F32)
    line = lax.broadcasted_iota(jnp.int32, (16, TILE), 0)
    below = jnp.zeros((16, TILE), F32)
    columns = []
    for k in range(4):
        row = jnp.where(half[0] == 0, all_rows[2 * k : 2 * k + 1], all_rows[2 * k + 1 : 2 * k + 2])
        below = jnp.where(line == k, jnp.broadcast_to(row, (16, TILE)), below)
        columns.append(down(row))
    out[PIECE : PIECE + 16, :] = jnp.concatenate([below, below], 1).astype(BF16)
    for k in range(4):
        copy(k).wait()
        out[k * TILE : (k + 1) * TILE, :] = (columns[k] * tiles[k].astype(F32)).astype(BF16)


def share_body(replica, degrees, features, cotangent, scaled, cot, deg, tile, sems):
    at = pl.ds(pl.multiple_of(replica[0] * TILE, TILE), TILE)
    first = pltpu.make_async_copy(features.at[at], tile, sems.at[0])
    second = pltpu.make_async_copy(cotangent.at[at], cot, sems.at[1])
    first.start()
    second.start()
    line = lax.broadcasted_iota(jnp.int32, (8, TILE), 0)
    row = jnp.sum(jnp.where(line == replica[0], degrees[...].astype(F32), 0.0), 0, keepdims=True)
    column = down(row)
    deg[...] = column
    first.wait()
    scaled[...] = (column * tile[...].astype(F32)).astype(BF16)
    second.wait()


def assemble_body(count, core, y, odd, row, col, vals, own, other, dense, sems, out_sems):
    dense[...] = jnp.zeros_like(dense)
    total = count[0, 0] + count[0, 1] + count[0, 2] + count[0, 3]

    @pl.loop(0, total)
    def _(k):
        at = col[0, k]
        q, sub = at >> 3, at & 7
        parity, pair = sub & 1, sub >> 1
        place = (parity ^ core[0]) * 16 + order_of(apart_of(q, odd[0], y[0])) * 4 + pair
        rows = pl.ds(pl.multiple_of(row[0, k] * TILE, TILE), TILE)
        cols = pl.ds(pl.multiple_of(place * TILE, TILE), TILE)
        pltpu.make_async_copy(vals.at[0, k], dense.at[rows, cols], sems.at[k]).start()

    @pl.loop(0, total)
    def _(k):
        corner = (pl.ds(0, TILE), pl.ds(0, TILE))
        pltpu.make_async_copy(vals.at[0, k], dense.at[corner], sems.at[k]).wait()

    width = own.shape[1]
    halves = [
        pltpu.make_async_copy(dense.at[:, pl.ds(i * width, width)], out, out_sems.at[i])
        for i, out in enumerate((own, other))
    ]
    for half in halves:
        half.start()
    for half in halves:
        half.wait()


def assemble(count, ids, row, col, vals, rows, cols):
    half = jax.ShapeDtypeStruct((rows, cols), BF16)
    return pl.pallas_call(
        assemble_body,
        out_shape=(half, half),
        in_specs=[SMEM] * 6 + [HBM],
        out_specs=(HBM, HBM),
        scratch_shapes=[
            pltpu.VMEM((rows, 2 * cols), BF16),
            pltpu.SemaphoreType.DMA((vals.shape[1],)),
            pltpu.SemaphoreType.DMA((2,)),
        ],
        name="assemble",
    )(count, *ids, row, col, vals)


def middle_body(factor, parts, scaled, cot, deg, weight, activated, both):
    summed = parts[0].astype(F32)
    for s in range(1, ZL * X):
        summed += parts[s].astype(F32)
    column = deg[...]
    propagated = (column * (summed + scaled[...].astype(F32))).astype(BF16)
    preact = jnp.dot(propagated, weight[...], preferred_element_type=F32)
    gate = jax.nn.sigmoid(preact)
    activated[...] = (preact * gate).astype(BF16)
    grad_pre = (cot[...].astype(F32) * gate * (1.0 + preact * (1.0 - gate))).astype(BF16)
    back = lax.dot_general(grad_pre, weight[...], (((1,), (1,)), ((), ())), preferred_element_type=F32)
    back = (column * back).astype(BF16)
    grad = lax.dot_general(propagated, grad_pre, (((0,), (0,)), ((), ())), preferred_element_type=F32)
    grad = (grad * factor).astype(BF16)
    for s in range(ZL * X):
        part = s // X * 2 + s % 2
        both[s, :TILE, :] = back
        both[s, TILE:, :] = grad[part * WROWS : (part + 1) * WROWS]


def regroup(ids, parity, rows, both, outs, others):
    y, odd, owner, q_own = ids
    for i, out in enumerate(outs):
        pair = (y + (0, 3, 1, 2)[i]) & 3

        def load(q, at):
            place = order_of(apart_of(q, odd, y)) * 4 + pair
            part = rows[pl.ds(pl.multiple_of(place * TILE, TILE), TILE), :]
            if others is None:
                return part
            return part + others[pl.ds(pl.multiple_of(i * PIECE + at, TILE), TILE), :].astype(F32)

        for q in range(4):
            out[q * TILE : (q + 1) * TILE, :] = load(q, q * TILE).astype(out.dtype)

        @pl.when(owner != 0)
        def _():
            at = pl.multiple_of(q_own * TILE, TILE)
            mine = load(q_own, at) + both[2 * pair + parity, :TILE, :].astype(F32)
            out[pl.ds(at, TILE), :] = mine.astype(out.dtype)


def slice_sum(both):
    total = both[0, TILE:, :].astype(F32)
    for s in range(1, ZL * X):
        total += both[s, TILE:, :].astype(F32)
    return total.astype(BF16)


def send_body(core, y, odd, owner, q_own, rows, both, out):
    outs = [out.at[i * PIECE : (i + 1) * PIECE] for i in range(4)]
    regroup((y[0], odd[0], owner[0], q_own[0]), 1 - core[0], rows, both, outs, None)
    out[4 * PIECE :, :] = slice_sum(both)


def keep_body(core, y, odd, owner, q_own, rows, both, others, keep, behind, ahead, up, down_, w_own, far):
    regroup((y[0], odd[0], owner[0], q_own[0]), core[0], rows, both, (keep, behind, ahead, far), others)
    for i, out in enumerate((up, down_)):
        out[...] = far[i * HALF : (i + 1) * HALF, :]
    w_own[...] = (slice_sum(both).astype(F32) + others[4 * PIECE :, :].astype(F32)).astype(BF16)


def relay_body(behind, ahead, up, down_, mine, came1, came2, came3, up_out, down_out, w_out):
    for i, (rows, came, out) in enumerate(((ahead, up, up_out), (behind, down_, down_out))):
        for k in range(2):
            part = slice(k * HALF, (k + 1) * HALF)
            value = rows[part, :]
            if k == i:
                value += came[...].astype(F32)
            out[part, :] = value.astype(BF16)
    total = mine[...].astype(F32) + came1[...].astype(F32)
    w_out[...] = total + (came2[...].astype(F32) + came3[...].astype(F32))


def spread_body(zh, keep, up2, down2, own, out1, out2, out3):
    for m, out in enumerate((own, out1, out2, out3)):
        at = pl.ds(pl.multiple_of((zh[0] ^ m) * TILE, TILE), TILE)
        chunk = keep[at, :] + up2[at, :].astype(F32) + down2[at, :].astype(F32)
        out[...] = chunk.astype(out.dtype)


def pass_body(source, out):
    out[...] = source[...]


def add_body(mine, came1, came2, came3, after, out):
    total = mine[...].astype(F32) + came1[...].astype(F32)
    out[...] = total + (came2[...].astype(F32) + came3[...].astype(F32))


def last_body(y, odd, zh, own, came1, came2, came3, p0, p1, p2, p3, grad):
    order = order_of(apart_of(zh[0], odd[0], y[0]))
    below = jnp.zeros((16, TILE), F32)
    for i, piece in enumerate((p0, p1, p2, p3)):
        below = jnp.where(order == i, piece[piece.shape[0] - 16 :, :TILE].astype(F32), below)
    line = lax.broadcasted_iota(jnp.int32, (16, TILE), 0)
    row = jnp.sum(jnp.where(line == y[0], below, 0.0), 0, keepdims=True)
    total = own[...]
    for came in (came1, came2, came3):
        total += came[...].astype(F32)
    grad[...] = (down(row) * total).astype(BF16)


def join_body(zl, xl, mine, over_z, over_x, over_both, out):
    for part, flip_z, flip_x in ((mine, 0, 0), (over_z, 1, 0), (over_x, 0, 1), (over_both, 1, 1)):
        at = ((zl[0] ^ flip_z) * 2 + (xl[0] ^ flip_x)) * WROWS
        out[pl.ds(pl.multiple_of(at, WROWS), WROWS), :] = part[...]


def shards(features, inv_sqrt_degree, weight, tile_vals, tile_row, tile_col, tile_count, cotangent):
    nodes_block, width = features.shape
    zh, y, core, zl, x = (lax.axis_index(a).reshape(1) for a in ALL)
    replica, block = lax.axis_index(REP), lax.axis_index(ROWS)
    nodes = nodes_block * ZH * Y * C
    cols = Y * PIECE
    odd = x & 1
    degrees = inv_sqrt_degree.reshape(nodes_block // TILE, TILE)

    def held(rows, kind=BF16):
        return pltpu.VMEM((rows, width), kind)

    piece = call(
        piece_body, "piece", held(PIECE + 16), [(x + (y >> 1)) & 1], [degrees, features], [WHOLE, HBM],
        [pltpu.VMEM((4, TILE, width), BF16), pltpu.SemaphoreType.DMA((4,))], LIMIT,
    )
    piece = lax.ppermute(piece, ALL, piece_route())
    scaled, cot, deg = call(
        share_body, "share", (held(TILE), held(TILE), held(TILE, F32)), [replica.reshape(1)],
        [degrees, features, cotangent], [WHOLE, HBM, HBM],
        [pltpu.VMEM((TILE, width), BF16), pltpu.SemaphoreType.DMA((2,))], LIMIT,
    )
    own_a, other_a = assemble(tile_count, [core, y, odd], tile_row, tile_col, tile_vals, nodes_block, cols)
    piece, own_a, other_a = lax.optimization_barrier((piece, own_a, other_a))

    swap = [(0, 1), (1, 0)]
    ahead, behind = ring_route(1), ring_route(-1)
    partial = jnp.dot(own_a[:, :PIECE], piece[:PIECE], preferred_element_type=F32)
    first = lax.ppermute(piece, "y", ahead)
    second = lax.ppermute(piece, "y", behind)
    third = lax.ppermute(first[:HALF], "y", ahead)
    fourth = lax.ppermute(second[HALF:], "y", behind)
    pieces = [piece, first, second, fourth]
    at = 0
    for own_x in (piece, first, second, third, fourth):
        other_x = lax.ppermute(own_x, "c", swap)
        size = own_x.shape[0] // TILE * TILE
        if at:
            partial = partial + jnp.dot(own_a[:, at : at + size], own_x[:size], preferred_element_type=F32)
        partial = partial + jnp.dot(other_a[:, at : at + size], other_x[:size], preferred_element_type=F32)
        at += size
    partial = partial.astype(BF16)
    owner, q_own = (replica == block // 4).astype(jnp.int32).reshape(1), (block % 4).reshape(1)
    partial, scaled, cot, deg, owner, q_own = lax.optimization_barrier(
        (partial, scaled, cot, deg, owner, q_own)
    )
    parts = lax.all_to_all(partial.reshape(ZL * X, TILE, width), REP, 0, 0)
    activated, both = call(
        lambda *refs: middle_body(float(nodes) ** -0.5, *refs),
        "middle",
        (jax.ShapeDtypeStruct((TILE, width), BF16), pltpu.VMEM((ZL * X, TILE + WROWS, width), BF16)),
        [],
        [parts, scaled, cot, deg, weight],
    )
    both = lax.all_to_all(both, REP, 0, 0)
    back_block = both[:, :TILE].reshape(nodes_block, width)
    ids = [core, y, odd, owner, q_own]

    def pull(a):
        return lax.dot_general(a, back_block, (((0,), (0,)), ((), ())), preferred_element_type=F32)

    others = call(send_body, "regroup_send", held(cols + WROWS), ids, [pull(other_a), both])
    others = lax.ppermute(others, "c", swap)
    keep, behind_rows, ahead_rows, up, down_, w_own = call(
        keep_body,
        "regroup_keep",
        (held(PIECE, F32), held(PIECE, F32), held(PIECE, F32), held(HALF), held(HALF), held(WROWS)),
        ids,
        [pull(own_a), both, others],
        scratch=[held(PIECE)],
    )
    up, down_ = lax.ppermute(up, "y", ahead), lax.ppermute(down_, "y", behind)
    w_rows = call(pass_body, "slices", held(WROWS), [], [w_own])
    w_y = [lax.ppermute(w_rows, "y", ring_route(m)) for m in range(1, 4)]
    up2, down2, w_rows = call(
        relay_body,
        "relay",
        (held(PIECE), held(PIECE), held(WROWS, F32)),
        [],
        [behind_rows, ahead_rows, up, down_, w_rows, *w_y],
    )
    up2, down2 = lax.ppermute(up2, "y", ahead), lax.ppermute(down2, "y", behind)
    w_rows = call(pass_body, "slices_y", held(WROWS, F32), [], [w_rows])
    exchange = [[(i, i ^ m) for i in range(ZH)] for m in range(1, 4)]
    w_z = [lax.ppermute(w_rows, "zh", route) for route in exchange]
    own, *sent = call(
        spread_body,
        "spread",
        (held(TILE, F32), held(TILE), held(TILE), held(TILE)),
        [zh],
        [keep, up2, down2],
    )
    w_mine = call(add_body, "slices_z", held(WROWS, F32), [], [w_rows, *w_z, sent[0]])
    got = [lax.ppermute(part, "zh", route) for part, route in zip(sent, exchange)]
    feature_grad = call(
        last_body,
        "last",
        jax.ShapeDtypeStruct((TILE, width), BF16),
        [y, odd, zh],
        [own, *got, *pieces],
    )
    flip = [(i, i ^ 1) for i in range(X)]
    over_z = lax.ppermute(w_mine, "zl", swap)
    over_x = lax.ppermute(w_mine, "x", flip)
    over_both = lax.ppermute(w_mine, REP, [(i, i ^ 5) for i in range(ZL * X)])
    weight_grad = call(
        join_body,
        "join",
        jax.ShapeDtypeStruct((width, width), F32),
        [zl, x & 1],
        [w_mine, over_z, over_x, over_both],
    )
    return (activated, weight_grad, feature_grad)


def solution(mesh):
    fine = Mesh(mesh.devices.reshape(ZH, Y, C, ZL, X), ALL)
    placed = (
        P(ROWS, None),
        P(ROWS),
        P(),
        P(ROWS, REP, None, None),
        P(ROWS, REP),
        P(ROWS, REP),
        P(ROWS, REP),
        P(ROWS, None),
    )
    return jax.shard_map(
        shards,
        mesh=fine,
        in_specs=placed,
        out_specs=(P(ALL, None), P(), P(REP + ROWS, None)),
        check_vma=False,
    )
```

```python
import jax
import jax.numpy as jnp
from jax import lax
from jax.experimental import pallas as pl
from jax.experimental.pallas import tpu as pltpu
from jax.sharding import Mesh, PartitionSpec as P

ZH, Y, C, ZL, X = 4, 4, 2, 2, 4
ROWS = ("zh", "y", "c")
REP = ("zl", "x")
ALL = ROWS + REP
TILE = 128
PIECE = 4 * TILE
HALF = 2 * TILE
WROWS = 64
LIMIT = None
BF16, F32 = jnp.bfloat16, jnp.float32
SMEM = pl.BlockSpec(memory_space=pltpu.SMEM)
WHOLE = pl.BlockSpec(memory_space=pltpu.VMEM)
HBM = pl.BlockSpec(memory_space=pltpu.HBM)


def flat(zh, y, c, zl, x):
    return (((zh * Y + y) * C + c) * ZL + zl) * X + x


def place_of(q, r):
    return (2 * (r % 2) + q // 2 + (q % 2) * (2 * (q // 2) - 1)) % Y


def piece_route():
    pairs = []
    for j in range(ZH * Y * C):
        for k in range(ZL * X):
            r = j // 4
            dx = (k % X - r % X) % X
            if k // X == r // X:
                near, far = 0, 3 if r // X == 0 else 1
            else:
                near, far = 1 if r // X == 0 else 3, 2
            zh = (j // (Y * C) + (far if dx < 2 else near)) % ZH
            pairs.append((j * (ZL * X) + k, flat(zh, place_of(j % 4, r), dx % 2, r // X, r % X)))
    return pairs


def ring_route(step):
    return [(y, (y + step) % Y) for y in range(Y)]


def order_of(apart):
    return jnp.where((apart & 1) == 0, 3 * (apart >> 1), 1 + ((3 - apart) >> 1))


def apart_of(q, odd, y):
    high, low = q >> 1, q & 1
    return (2 * odd + high + low * (2 * high - 1) - y) & 3


def down(row):
    square = jnp.transpose(jnp.broadcast_to(row, (TILE, TILE)))
    return jnp.concatenate([square, square], 1)


def call(body, name, outs, scalars, arrays, specs=None, scratch=(), limit=16 << 20):
    return pl.pallas_call(
        body,
        out_shape=outs,
        in_specs=[SMEM] * len(scalars) + (specs or [WHOLE] * len(arrays)),
        out_specs=jax.tree.map(lambda _: WHOLE, outs),
        scratch_shapes=list(scratch),
        compiler_params=pltpu.CompilerParams(vmem_limit_bytes=limit),
        name=name,
    )(*scalars, *arrays)


def piece_body(half, degrees, features, out, tiles, near, sems):
    def copy(k):
        at = pl.ds(pl.multiple_of((2 * k + half[0]) * TILE, TILE), TILE)
        return pltpu.make_async_copy(features.at[at], tiles.at[k], sems.at[k])

    fetch = pltpu.make_async_copy(degrees, near, sems.at[4])
    fetch.start()
    for k in range(4):
        copy(k).start()
    fetch.wait()
    all_rows = near[...].astype(F32)
    line = lax.broadcasted_iota(jnp.int32, (16, TILE), 0)
    below = jnp.zeros((16, TILE), F32)
    columns = []
    for k in range(4):
        row = jnp.where(half[0] == 0, all_rows[2 * k : 2 * k + 1], all_rows[2 * k + 1 : 2 * k + 2])
        below = jnp.where(line == k, jnp.broadcast_to(row, (16, TILE)), below)
        columns.append(down(row))
    out[PIECE : PIECE + 16, :] = jnp.concatenate([below, below], 1).astype(BF16)
    for k in range(4):
        copy(k).wait()
        out[k * TILE : (k + 1) * TILE, :] = (columns[k] * tiles[k].astype(F32)).astype(BF16)


def share_body(replica, degrees, features, cotangent, scaled, cot, deg, tile, sems):
    at = pl.ds(pl.multiple_of(replica[0] * TILE, TILE), TILE)
    first = pltpu.make_async_copy(features.at[at], tile, sems.at[0])
    second = pltpu.make_async_copy(cotangent.at[at], cot, sems.at[1])
    first.start()
    second.start()
    line = lax.broadcasted_iota(jnp.int32, (8, TILE), 0)
    row = jnp.sum(jnp.where(line == replica[0], degrees[...].astype(F32), 0.0), 0, keepdims=True)
    column = down(row)
    deg[...] = column
    first.wait()
    scaled[...] = (column * tile[...].astype(F32)).astype(BF16)
    second.wait()


def assemble_body(count, core, y, odd, row, col, vals, own, other, dense, sems, out_sems):
    dense[...] = jnp.zeros_like(dense)
    total = count[0, 0] + count[0, 1] + count[0, 2] + count[0, 3]

    @pl.loop(0, total)
    def _(k):
        at = col[0, k]
        q, sub = at >> 3, at & 7
        parity, pair = sub & 1, sub >> 1
        place = (parity ^ core[0]) * 16 + order_of(apart_of(q, odd[0], y[0])) * 4 + pair
        rows = pl.ds(pl.multiple_of(row[0, k] * TILE, TILE), TILE)
        cols = pl.ds(pl.multiple_of(place * TILE, TILE), TILE)
        pltpu.make_async_copy(vals.at[0, k], dense.at[rows, cols], sems.at[k]).start()

    @pl.loop(0, total)
    def _(k):
        corner = (pl.ds(0, TILE), pl.ds(0, TILE))
        pltpu.make_async_copy(vals.at[0, k], dense.at[corner], sems.at[k]).wait()

    width = own.shape[1]
    halves = [
        pltpu.make_async_copy(dense.at[:, pl.ds(i * width, width)], out, out_sems.at[i])
        for i, out in enumerate((own, other))
    ]
    for half in halves:
        half.start()
    for half in halves:
        half.wait()


def assemble(count, ids, row, col, vals, rows, cols):
    half = jax.ShapeDtypeStruct((rows, cols), BF16)
    return pl.pallas_call(
        assemble_body,
        out_shape=(half, half),
        in_specs=[SMEM] * 6 + [HBM],
        out_specs=(HBM, HBM),
        scratch_shapes=[
            pltpu.VMEM((rows, 2 * cols), BF16),
            pltpu.SemaphoreType.DMA((vals.shape[1],)),
            pltpu.SemaphoreType.DMA((2,)),
        ],
        name="assemble",
    )(count, *ids, row, col, vals)


def middle_body(factor, parts, scaled, cot, deg, weight, activated, both):
    summed = parts[0].astype(F32)
    for s in range(1, ZL * X):
        summed += parts[s].astype(F32)
    column = deg[...]
    propagated = (column * (summed + scaled[...].astype(F32))).astype(BF16)
    preact = jnp.dot(propagated, weight[...], preferred_element_type=F32)
    gate = jax.nn.sigmoid(preact)
    activated[...] = (preact * gate).astype(BF16)
    grad_pre = (cot[...].astype(F32) * gate * (1.0 + preact * (1.0 - gate))).astype(BF16)
    back = lax.dot_general(grad_pre, weight[...], (((1,), (1,)), ((), ())), preferred_element_type=F32)
    back = (column * back).astype(BF16)
    grad = lax.dot_general(propagated, grad_pre, (((0,), (0,)), ((), ())), preferred_element_type=F32)
    grad = (grad * factor).astype(BF16)
    for s in range(ZL * X):
        part = s // X * 2 + s % 2
        both[s, :TILE, :] = back
        both[s, TILE:, :] = grad[part * WROWS : (part + 1) * WROWS]


def regroup(ids, parity, rows, both, outs, others):
    y, odd, owner, q_own = ids
    for i, out in enumerate(outs):
        pair = (y + (0, 3, 1, 2)[i]) & 3

        def load(q, at):
            place = order_of(apart_of(q, odd, y)) * 4 + pair
            part = rows[pl.ds(pl.multiple_of(place * TILE, TILE), TILE), :]
            if others is None:
                return part
            return part + others[pl.ds(pl.multiple_of(i * PIECE + at, TILE), TILE), :].astype(F32)

        for q in range(4):
            out[q * TILE : (q + 1) * TILE, :] = load(q, q * TILE).astype(out.dtype)

        @pl.when(owner != 0)
        def _():
            at = pl.multiple_of(q_own * TILE, TILE)
            mine = load(q_own, at) + both[2 * pair + parity, :TILE, :].astype(F32)
            out[pl.ds(at, TILE), :] = mine.astype(out.dtype)


def slice_sum(both):
    total = both[0, TILE:, :].astype(F32)
    for s in range(1, ZL * X):
        total += both[s, TILE:, :].astype(F32)
    return total.astype(BF16)


def send_body(core, y, odd, owner, q_own, rows, both, out):
    outs = [out.at[i * PIECE : (i + 1) * PIECE] for i in range(4)]
    regroup((y[0], odd[0], owner[0], q_own[0]), 1 - core[0], rows, both, outs, None)
    out[4 * PIECE :, :] = slice_sum(both)


def keep_body(core, y, odd, owner, q_own, rows, both, others, keep, behind, ahead, up, down_, w_own, far):
    regroup((y[0], odd[0], owner[0], q_own[0]), core[0], rows, both, (keep, behind, ahead, far), others)
    for i, out in enumerate((up, down_)):
        out[...] = far[i * HALF : (i + 1) * HALF, :]
    w_own[...] = (slice_sum(both).astype(F32) + others[4 * PIECE :, :].astype(F32)).astype(BF16)


def relay_body(behind, ahead, up, down_, mine, came1, came2, came3, up_out, down_out, w_out):
    for i, (rows, came, out) in enumerate(((ahead, up, up_out), (behind, down_, down_out))):
        for k in range(2):
            part = slice(k * HALF, (k + 1) * HALF)
            value = rows[part, :]
            if k == i:
                value += came[...].astype(F32)
            out[part, :] = value.astype(BF16)
    total = mine[...].astype(F32) + came1[...].astype(F32)
    w_out[...] = total + (came2[...].astype(F32) + came3[...].astype(F32))


def spread_body(zh, keep, up2, down2, own, out1, out2, out3):
    for m, out in enumerate((own, out1, out2, out3)):
        at = pl.ds(pl.multiple_of((zh[0] ^ m) * TILE, TILE), TILE)
        chunk = keep[at, :] + up2[at, :].astype(F32) + down2[at, :].astype(F32)
        out[...] = chunk.astype(out.dtype)


def pass_body(source, out):
    out[...] = source[...]


def add_body(mine, came1, came2, came3, after, out):
    total = mine[...].astype(F32) + came1[...].astype(F32)
    out[...] = total + (came2[...].astype(F32) + came3[...].astype(F32))


def last_body(y, odd, zh, own, came1, came2, came3, p0, p1, p2, p3, grad):
    order = order_of(apart_of(zh[0], odd[0], y[0]))
    below = jnp.zeros((16, TILE), F32)
    for i, piece in enumerate((p0, p1, p2, p3)):
        below = jnp.where(order == i, piece[piece.shape[0] - 16 :, :TILE].astype(F32), below)
    line = lax.broadcasted_iota(jnp.int32, (16, TILE), 0)
    row = jnp.sum(jnp.where(line == y[0], below, 0.0), 0, keepdims=True)
    total = own[...]
    for came in (came1, came2, came3):
        total += came[...].astype(F32)
    grad[...] = (down(row) * total).astype(BF16)


def join_body(zl, xl, mine, over_z, over_x, over_both, out):
    for part, flip_z, flip_x in ((mine, 0, 0), (over_z, 1, 0), (over_x, 0, 1), (over_both, 1, 1)):
        at = ((zl[0] ^ flip_z) * 2 + (xl[0] ^ flip_x)) * WROWS
        out[pl.ds(pl.multiple_of(at, WROWS), WROWS), :] = part[...]


def shards(features, inv_sqrt_degree, weight, tile_vals, tile_row, tile_col, tile_count, cotangent):
    nodes_block, width = features.shape
    zh, y, core, zl, x = (lax.axis_index(a).reshape(1) for a in ALL)
    replica, block = lax.axis_index(REP), lax.axis_index(ROWS)
    nodes = nodes_block * ZH * Y * C
    cols = Y * PIECE
    odd = x & 1
    degrees = inv_sqrt_degree.reshape(nodes_block // TILE, TILE)

    def held(rows, kind=BF16):
        return pltpu.VMEM((rows, width), kind)

    piece = call(
        piece_body, "piece", held(PIECE + 16), [(x + (y >> 1)) & 1], [degrees, features], [HBM, HBM],
        [
            pltpu.VMEM((4, TILE, width), BF16),
            pltpu.VMEM(degrees.shape, BF16),
            pltpu.SemaphoreType.DMA((5,)),
        ],
        LIMIT,
    )
    piece = lax.ppermute(piece, ALL, piece_route())
    scaled, cot, deg = call(
        share_body, "share", (held(TILE), held(TILE), held(TILE, F32)), [replica.reshape(1)],
        [degrees, features, cotangent], [WHOLE, HBM, HBM],
        [pltpu.VMEM((TILE, width), BF16), pltpu.SemaphoreType.DMA((2,))], LIMIT,
    )
    own_a, other_a = assemble(tile_count, [core, y, odd], tile_row, tile_col, tile_vals, nodes_block, cols)
    piece, own_a, other_a = lax.optimization_barrier((piece, own_a, other_a))

    swap = [(0, 1), (1, 0)]
    ahead, behind = ring_route(1), ring_route(-1)
    partial = jnp.dot(own_a[:, :PIECE], piece[:PIECE], preferred_element_type=F32)
    first = lax.ppermute(piece, "y", ahead)
    second = lax.ppermute(piece, "y", behind)
    third = lax.ppermute(first[:HALF], "y", ahead)
    fourth = lax.ppermute(second[HALF:], "y", behind)
    pieces = [piece, first, second, fourth]
    at = 0
    for own_x in (piece, first, second, third, fourth):
        other_x = lax.ppermute(own_x, "c", swap)
        size = own_x.shape[0] // TILE * TILE
        if at:
            partial = partial + jnp.dot(own_a[:, at : at + size], own_x[:size], preferred_element_type=F32)
        partial = partial + jnp.dot(other_a[:, at : at + size], other_x[:size], preferred_element_type=F32)
        at += size
    partial = partial.astype(BF16)
    owner, q_own = (replica == block // 4).astype(jnp.int32).reshape(1), (block % 4).reshape(1)
    partial, scaled, cot, deg, owner, q_own = lax.optimization_barrier(
        (partial, scaled, cot, deg, owner, q_own)
    )
    parts = lax.all_to_all(partial.reshape(ZL * X, TILE, width), REP, 0, 0)
    activated, both = call(
        lambda *refs: middle_body(float(nodes) ** -0.5, *refs),
        "middle",
        (jax.ShapeDtypeStruct((TILE, width), BF16), pltpu.VMEM((ZL * X, TILE + WROWS, width), BF16)),
        [],
        [parts, scaled, cot, deg, weight],
    )
    both = lax.all_to_all(both, REP, 0, 0)
    back_block = both[:, :TILE].reshape(nodes_block, width)
    ids = [core, y, odd, owner, q_own]

    def pull(a):
        return lax.dot_general(a, back_block, (((0,), (0,)), ((), ())), preferred_element_type=F32)

    others = call(send_body, "regroup_send", held(cols + WROWS), ids, [pull(other_a), both])
    others = lax.ppermute(others, "c", swap)
    keep, behind_rows, ahead_rows, up, down_, w_own = call(
        keep_body,
        "regroup_keep",
        (held(PIECE, F32), held(PIECE, F32), held(PIECE, F32), held(HALF), held(HALF), held(WROWS)),
        ids,
        [pull(own_a), both, others],
        scratch=[held(PIECE)],
    )
    up, down_ = lax.ppermute(up, "y", ahead), lax.ppermute(down_, "y", behind)
    w_rows = call(pass_body, "slices", held(WROWS), [], [w_own])
    w_y = [lax.ppermute(w_rows, "y", ring_route(m)) for m in range(1, 4)]
    up2, down2, w_rows = call(
        relay_body,
        "relay",
        (held(PIECE), held(PIECE), held(WROWS, F32)),
        [],
        [behind_rows, ahead_rows, up, down_, w_rows, *w_y],
    )
    up2, down2 = lax.ppermute(up2, "y", ahead), lax.ppermute(down2, "y", behind)
    w_rows = call(pass_body, "slices_y", held(WROWS, F32), [], [w_rows])
    exchange = [[(i, i ^ m) for i in range(ZH)] for m in range(1, 4)]
    w_z = [lax.ppermute(w_rows, "zh", route) for route in exchange]
    own, *sent = call(
        spread_body,
        "spread",
        (held(TILE, F32), held(TILE), held(TILE), held(TILE)),
        [zh],
        [keep, up2, down2],
    )
    w_mine = call(add_body, "slices_z", held(WROWS, F32), [], [w_rows, *w_z, sent[0]])
    got = [lax.ppermute(part, "zh", route) for part, route in zip(sent, exchange)]
    feature_grad = call(
        last_body,
        "last",
        jax.ShapeDtypeStruct((TILE, width), BF16),
        [y, odd, zh],
        [own, *got, *pieces],
    )
    flip = [(i, i ^ 1) for i in range(X)]
    over_z = lax.ppermute(w_mine, "zl", swap)
    over_x = lax.ppermute(w_mine, "x", flip)
    over_both = lax.ppermute(w_mine, REP, [(i, i ^ 5) for i in range(ZL * X)])
    weight_grad = call(
        join_body,
        "join",
        jax.ShapeDtypeStruct((width, width), F32),
        [zl, x & 1],
        [w_mine, over_z, over_x, over_both],
    )
    return (activated, weight_grad, feature_grad)


def solution(mesh):
    fine = Mesh(mesh.devices.reshape(ZH, Y, C, ZL, X), ALL)
    placed = (
        P(ROWS, None),
        P(ROWS),
        P(),
        P(ROWS, REP, None, None),
        P(ROWS, REP),
        P(ROWS, REP),
        P(ROWS, REP),
        P(ROWS, None),
    )
    return jax.shard_map(
        shards,
        mesh=fine,
        in_specs=placed,
        out_specs=(P(ALL, None), P(), P(REP + ROWS, None)),
        check_vma=False,
    )
```

```python
import jax
import jax.numpy as jnp
from jax import lax
from jax.experimental import pallas as pl
from jax.experimental.pallas import tpu as pltpu
from jax.sharding import Mesh, PartitionSpec as P

ZH, Y, C, ZL, X = 4, 4, 2, 2, 4
ROWS = ("zh", "y", "c")
REP = ("zl", "x")
ALL = ROWS + REP
TILE = 128
PIECE = 4 * TILE
HALF = 2 * TILE
WROWS = 64
LIMIT = None
BF16, F32 = jnp.bfloat16, jnp.float32
SMEM = pl.BlockSpec(memory_space=pltpu.SMEM)
WHOLE = pl.BlockSpec(memory_space=pltpu.VMEM)
HBM = pl.BlockSpec(memory_space=pltpu.HBM)


def flat(zh, y, c, zl, x):
    return (((zh * Y + y) * C + c) * ZL + zl) * X + x


def place_of(q, r):
    return (2 * (r % 2) + q // 2 + (q % 2) * (2 * (q // 2) - 1)) % Y


def piece_route():
    pairs = []
    for j in range(ZH * Y * C):
        for k in range(ZL * X):
            r = j // 4
            dx = (k % X - r % X) % X
            if k // X == r // X:
                near, far = 0, 3 if r // X == 0 else 1
            else:
                near, far = 1 if r // X == 0 else 3, 2
            zh = (j // (Y * C) + (far if dx < 2 else near)) % ZH
            pairs.append((j * (ZL * X) + k, flat(zh, place_of(j % 4, r), dx % 2, r // X, r % X)))
    return pairs


def ring_route(step):
    return [(y, (y + step) % Y) for y in range(Y)]


def order_of(apart):
    return jnp.where((apart & 1) == 0, 3 * (apart >> 1), 1 + ((3 - apart) >> 1))


def apart_of(q, odd, y):
    high, low = q >> 1, q & 1
    return (2 * odd + high + low * (2 * high - 1) - y) & 3


def down(row):
    square = jnp.transpose(jnp.broadcast_to(row, (TILE, TILE)))
    return jnp.concatenate([square, square], 1)


def call(body, name, outs, scalars, arrays, specs=None, scratch=(), limit=16 << 20):
    return pl.pallas_call(
        body,
        out_shape=outs,
        in_specs=[SMEM] * len(scalars) + (specs or [WHOLE] * len(arrays)),
        out_specs=jax.tree.map(lambda _: WHOLE, outs),
        scratch_shapes=list(scratch),
        compiler_params=pltpu.CompilerParams(vmem_limit_bytes=limit),
        name=name,
    )(*scalars, *arrays)


def piece_body(half, degrees, features, out, tiles, near, sems):
    def copy(k):
        at = pl.ds(pl.multiple_of((2 * k + half[0]) * TILE, TILE), TILE)
        return pltpu.make_async_copy(features.at[at], tiles.at[k], sems.at[k])

    fetch = pltpu.make_async_copy(degrees, near, sems.at[4])
    fetch.start()
    for k in range(4):
        copy(k).start()
    fetch.wait()
    all_rows = near[...].astype(F32)
    line = lax.broadcasted_iota(jnp.int32, (16, TILE), 0)
    below = jnp.zeros((16, TILE), F32)
    columns = []
    for k in range(4):
        row = jnp.where(half[0] == 0, all_rows[2 * k : 2 * k + 1], all_rows[2 * k + 1 : 2 * k + 2])
        below = jnp.where(line == k, jnp.broadcast_to(row, (16, TILE)), below)
        columns.append(down(row))
    out[PIECE : PIECE + 16, :] = jnp.concatenate([below, below], 1).astype(BF16)
    for k in range(4):
        copy(k).wait()
        out[k * TILE : (k + 1) * TILE, :] = (columns[k] * tiles[k].astype(F32)).astype(BF16)


def share_body(replica, degrees, features, cotangent, scaled, cot, deg, tile, sems):
    at = pl.ds(pl.multiple_of(replica[0] * TILE, TILE), TILE)
    first = pltpu.make_async_copy(features.at[at], tile, sems.at[0])
    second = pltpu.make_async_copy(cotangent.at[at], cot, sems.at[1])
    first.start()
    second.start()
    line = lax.broadcasted_iota(jnp.int32, (8, TILE), 0)
    row = jnp.sum(jnp.where(line == replica[0], degrees[...].astype(F32), 0.0), 0, keepdims=True)
    column = down(row)
    deg[...] = column
    first.wait()
    scaled[...] = (column * tile[...].astype(F32)).astype(BF16)
    second.wait()


def assemble_body(count, core, y, odd, row, col, vals, own, other, dense, sems, out_sems):
    dense[...] = jnp.zeros_like(dense)
    total = count[0, 0] + count[0, 1] + count[0, 2] + count[0, 3]

    @pl.loop(0, total)
    def _(k):
        at = col[0, k]
        q, sub = at >> 3, at & 7
        parity, pair = sub & 1, sub >> 1
        place = (parity ^ core[0]) * 16 + order_of(apart_of(q, odd[0], y[0])) * 4 + pair
        rows = pl.ds(pl.multiple_of(row[0, k] * TILE, TILE), TILE)
        cols = pl.ds(pl.multiple_of(place * TILE, TILE), TILE)
        pltpu.make_async_copy(vals.at[0, k], dense.at[rows, cols], sems.at[k]).start()

    @pl.loop(0, total)
    def _(k):
        corner = (pl.ds(0, TILE), pl.ds(0, TILE))
        pltpu.make_async_copy(vals.at[0, k], dense.at[corner], sems.at[k]).wait()

    width = own.shape[1]
    halves = [
        pltpu.make_async_copy(dense.at[:, pl.ds(i * width, width)], out, out_sems.at[i])
        for i, out in enumerate((own, other))
    ]
    for half in halves:
        half.start()
    for half in halves:
        half.wait()


def assemble(count, ids, row, col, vals, rows, cols):
    half = jax.ShapeDtypeStruct((rows, cols), BF16)
    return pl.pallas_call(
        assemble_body,
        out_shape=(half, half),
        in_specs=[SMEM] * 6 + [HBM],
        out_specs=(HBM, HBM),
        scratch_shapes=[
            pltpu.VMEM((rows, 2 * cols), BF16),
            pltpu.SemaphoreType.DMA((vals.shape[1],)),
            pltpu.SemaphoreType.DMA((2,)),
        ],
        name="assemble",
    )(count, *ids, row, col, vals)


def middle_body(factor, parts, scaled, cot, deg, weight, activated, both):
    summed = parts[0].astype(F32)
    for s in range(1, ZL * X):
        summed += parts[s].astype(F32)
    column = deg[...]
    propagated = (column * (summed + scaled[...].astype(F32))).astype(BF16)
    preact = jnp.dot(propagated, weight[...], preferred_element_type=F32)
    gate = jax.nn.sigmoid(preact)
    activated[...] = (preact * gate).astype(BF16)
    grad_pre = (cot[...].astype(F32) * gate * (1.0 + preact * (1.0 - gate))).astype(BF16)
    back = lax.dot_general(grad_pre, weight[...], (((1,), (1,)), ((), ())), preferred_element_type=F32)
    back = (column * back).astype(BF16)
    grad = lax.dot_general(propagated, grad_pre, (((0,), (0,)), ((), ())), preferred_element_type=F32)
    grad = (grad * factor).astype(BF16)
    for s in range(ZL * X):
        part = s // X * 2 + s % 2
        both[s, :TILE, :] = back
        both[s, TILE:, :] = grad[part * WROWS : (part + 1) * WROWS]


def regroup(ids, parity, rows, both, outs, others):
    y, odd, owner, q_own = ids
    for i, out in enumerate(outs):
        pair = (y + (0, 3, 1, 2)[i]) & 3

        def load(q, at):
            place = order_of(apart_of(q, odd, y)) * 4 + pair
            part = rows[pl.ds(pl.multiple_of(place * TILE, TILE), TILE), :]
            if others is None:
                return part
            return part + others[pl.ds(pl.multiple_of(i * PIECE + at, TILE), TILE), :].astype(F32)

        for q in range(4):
            out[q * TILE : (q + 1) * TILE, :] = load(q, q * TILE).astype(out.dtype)

        @pl.when(owner != 0)
        def _():
            at = pl.multiple_of(q_own * TILE, TILE)
            mine = load(q_own, at) + both[2 * pair + parity, :TILE, :].astype(F32)
            out[pl.ds(at, TILE), :] = mine.astype(out.dtype)


def slice_sum(both):
    total = both[0, TILE:, :].astype(F32)
    for s in range(1, ZL * X):
        total += both[s, TILE:, :].astype(F32)
    return total.astype(BF16)


def send_body(core, y, odd, owner, q_own, rows, both, out):
    outs = [out.at[i * PIECE : (i + 1) * PIECE] for i in range(4)]
    regroup((y[0], odd[0], owner[0], q_own[0]), 1 - core[0], rows, both, outs, None)
    out[4 * PIECE :, :] = slice_sum(both)


def keep_body(core, y, odd, owner, q_own, rows, both, others, keep, behind, ahead, up, down_, w_own, far):
    regroup((y[0], odd[0], owner[0], q_own[0]), core[0], rows, both, (keep, behind, ahead, far), others)
    for i, out in enumerate((up, down_)):
        out[...] = far[i * HALF : (i + 1) * HALF, :]
    w_own[...] = (slice_sum(both).astype(F32) + others[4 * PIECE :, :].astype(F32)).astype(BF16)


def relay_body(behind, ahead, up, down_, mine, came1, came2, came3, up_out, down_out, w_out):
    for i, (rows, came, out) in enumerate(((ahead, up, up_out), (behind, down_, down_out))):
        for k in range(2):
            part = slice(k * HALF, (k + 1) * HALF)
            value = rows[part, :]
            if k == i:
                value += came[...].astype(F32)
            out[part, :] = value.astype(BF16)
    total = mine[...].astype(F32) + came1[...].astype(F32)
    w_out[...] = total + (came2[...].astype(F32) + came3[...].astype(F32))


def spread_body(zh, keep, up2, down2, own, out1, out2, out3):
    for m, out in enumerate((own, out1, out2, out3)):
        at = pl.ds(pl.multiple_of((zh[0] ^ m) * TILE, TILE), TILE)
        chunk = keep[at, :] + up2[at, :].astype(F32) + down2[at, :].astype(F32)
        out[...] = chunk.astype(out.dtype)


def pass_body(source, out):
    out[...] = source[...]


def add_body(mine, came1, came2, came3, after, out):
    total = mine[...].astype(F32) + came1[...].astype(F32)
    out[...] = total + (came2[...].astype(F32) + came3[...].astype(F32))


def last_body(y, odd, zh, own, came1, came2, came3, p0, p1, p2, p3, grad):
    order = order_of(apart_of(zh[0], odd[0], y[0]))
    below = jnp.zeros((16, TILE), F32)
    for i, piece in enumerate((p0, p1, p2, p3)):
        below = jnp.where(order == i, piece[piece.shape[0] - 16 :, :TILE].astype(F32), below)
    line = lax.broadcasted_iota(jnp.int32, (16, TILE), 0)
    row = jnp.sum(jnp.where(line == y[0], below, 0.0), 0, keepdims=True)
    total = own[...]
    for came in (came1, came2, came3):
        total += came[...].astype(F32)
    grad[...] = (down(row) * total).astype(BF16)


def join_body(zl, xl, mine, over_z, over_x, over_both, out):
    for part, flip_z, flip_x in ((mine, 0, 0), (over_z, 1, 0), (over_x, 0, 1), (over_both, 1, 1)):
        at = ((zl[0] ^ flip_z) * 2 + (xl[0] ^ flip_x)) * WROWS
        out[pl.ds(pl.multiple_of(at, WROWS), WROWS), :] = part[...]


def shards(features, inv_sqrt_degree, weight, tile_vals, tile_row, tile_col, tile_count, cotangent):
    nodes_block, width = features.shape
    zh, y, core, zl, x = (lax.axis_index(a).reshape(1) for a in ALL)
    replica, block = lax.axis_index(REP), lax.axis_index(ROWS)
    nodes = nodes_block * ZH * Y * C
    cols = Y * PIECE
    odd = x & 1
    degrees = inv_sqrt_degree.reshape(nodes_block // TILE, TILE)

    def held(rows, kind=BF16):
        return pltpu.VMEM((rows, width), kind)

    piece = call(
        piece_body, "piece", held(PIECE + 16), [(x + (y >> 1)) & 1], [degrees, features], [HBM, HBM],
        [
            pltpu.VMEM((4, TILE, width), BF16),
            pltpu.VMEM(degrees.shape, BF16),
            pltpu.SemaphoreType.DMA((5,)),
        ],
        LIMIT,
    )
    piece = lax.ppermute(piece, ALL, piece_route())
    scaled, cot, deg = call(
        share_body, "share", (held(TILE), held(TILE), held(TILE, F32)), [replica.reshape(1)],
        [degrees, features, cotangent], [WHOLE, HBM, HBM],
        [pltpu.VMEM((TILE, width), BF16), pltpu.SemaphoreType.DMA((2,))], LIMIT,
    )
    own_a, other_a = assemble(tile_count, [core, y, odd], tile_row, tile_col, tile_vals, nodes_block, cols)
    piece, own_a, other_a = lax.optimization_barrier((piece, own_a, other_a))

    swap = [(0, 1), (1, 0)]
    ahead, behind = ring_route(1), ring_route(-1)
    partial = jnp.dot(own_a[:, :PIECE], piece[:PIECE], preferred_element_type=F32)
    first = lax.ppermute(piece, "y", ahead)
    second = lax.ppermute(piece, "y", behind)
    third = lax.ppermute(first[:HALF], "y", ahead)
    fourth = lax.ppermute(second[HALF:], "y", behind)
    pieces = [piece, first, second, fourth]
    at = 0
    for own_x in (piece, first, second, third, fourth):
        other_x = lax.ppermute(own_x, "c", swap)
        size = own_x.shape[0] // TILE * TILE
        if at:
            partial = partial + jnp.dot(own_a[:, at : at + size], own_x[:size], preferred_element_type=F32)
        partial = partial + jnp.dot(other_a[:, at : at + size], other_x[:size], preferred_element_type=F32)
        at += size
    partial = partial.astype(BF16)
    owner, q_own = (replica == block // 4).astype(jnp.int32).reshape(1), (block % 4).reshape(1)
    partial, scaled, cot, deg, owner, q_own = lax.optimization_barrier(
        (partial, scaled, cot, deg, owner, q_own)
    )
    parts = lax.all_to_all(partial.reshape(ZL * X, TILE, width), REP, 0, 0)
    activated, both = call(
        lambda *refs: middle_body(float(nodes) ** -0.5, *refs),
        "middle",
        (jax.ShapeDtypeStruct((TILE, width), BF16), pltpu.VMEM((ZL * X, TILE + WROWS, width), BF16)),
        [],
        [parts, scaled, cot, deg, weight],
    )
    both = lax.all_to_all(both, REP, 0, 0)
    back_block = both[:, :TILE].reshape(nodes_block, width)
    ids = [core, y, odd, owner, q_own]

    def pull(a):
        return lax.dot_general(a, back_block, (((0,), (0,)), ((), ())), preferred_element_type=F32)

    others = call(send_body, "regroup_send", held(cols + WROWS), ids, [pull(other_a), both])
    others = lax.ppermute(others, "c", swap)
    keep, behind_rows, ahead_rows, up, down_, w_own = call(
        keep_body,
        "regroup_keep",
        (held(PIECE, F32), held(PIECE, F32), held(PIECE, F32), held(HALF), held(HALF), held(WROWS)),
        ids,
        [pull(own_a), both, others],
        scratch=[held(PIECE)],
    )
    up, down_ = lax.ppermute(up, "y", ahead), lax.ppermute(down_, "y", behind)
    w_rows = call(pass_body, "slices", held(WROWS), [], [w_own])
    w_y = [lax.ppermute(w_rows, "y", ring_route(m)) for m in (2, 1, 3)]
    up2, down2, w_rows = call(
        relay_body,
        "relay",
        (held(PIECE), held(PIECE), held(WROWS, F32)),
        [],
        [behind_rows, ahead_rows, up, down_, w_rows, *w_y],
    )
    up2, down2 = lax.ppermute(up2, "y", ahead), lax.ppermute(down2, "y", behind)
    w_rows = call(pass_body, "slices_y", held(WROWS, F32), [], [w_rows])
    exchange = [[(i, i ^ m) for i in range(ZH)] for m in range(1, 4)]
    w_z = [lax.ppermute(w_rows, "zh", route) for route in exchange]
    own, *sent = call(
        spread_body,
        "spread",
        (held(TILE, F32), held(TILE), held(TILE), held(TILE)),
        [zh],
        [keep, up2, down2],
    )
    w_mine = call(add_body, "slices_z", held(WROWS, F32), [], [w_rows, *w_z, sent[0]])
    got = [lax.ppermute(part, "zh", route) for part, route in zip(sent, exchange)]
    feature_grad = call(
        last_body,
        "last",
        jax.ShapeDtypeStruct((TILE, width), BF16),
        [y, odd, zh],
        [own, *got, *pieces],
    )
    flip = [(i, i ^ 1) for i in range(X)]
    over_z = lax.ppermute(w_mine, "zl", swap)
    over_x = lax.ppermute(w_mine, "x", flip)
    over_both = lax.ppermute(w_mine, REP, [(i, i ^ 5) for i in range(ZL * X)])
    weight_grad = call(
        join_body,
        "join",
        jax.ShapeDtypeStruct((width, width), F32),
        [zl, x & 1],
        [w_mine, over_z, over_x, over_both],
    )
    return (activated, weight_grad, feature_grad)


def solution(mesh):
    fine = Mesh(mesh.devices.reshape(ZH, Y, C, ZL, X), ALL)
    placed = (
        P(ROWS, None),
        P(ROWS),
        P(),
        P(ROWS, REP, None, None),
        P(ROWS, REP),
        P(ROWS, REP),
        P(ROWS, REP),
        P(ROWS, None),
    )
    return jax.shard_map(
        shards,
        mesh=fine,
        in_specs=placed,
        out_specs=(P(ALL, None), P(), P(REP + ROWS, None)),
        check_vma=False,
    )
```
